32 devices in a mesh: freq: 4 (over y, x), param: 8 (over z, core).
Axes of the slice: x: 2, y: 2, z: 4, core: 2. Of those that a mesh axis runs over, the one named last changes fastest.
Arguments:
- chain_state: float32 [32, 2048, 512], P('freq', 'param'), may hold values from -6 to 6
- second_moment: float32 [32, 2048, 512], P('freq', 'param'), may hold values from 0.25 to 2
- noise: float32 [2, 32, 2048, 512], P(None, 'freq', 'param'), may hold values from -6 to 6
- green: bfloat16 [2, 64, 2048, 512], P(None, 'freq', 'param'), may hold values from -0.125 to 0.125
- observed: float32 [64, 1024], P('freq'), may hold values from -6 to 6
- inv_noise: float32 [64, 512], P('freq'), may hold values from 0.3 to 3
- temper: float32 [32], P('freq'), may hold values from 0.2 to 1
Outputs:
- new_state: float32 [32, 2048, 512], P('freq', 'param')
- new_moment: float32 [32, 2048, 512], P('freq', 'param')
The draws below stay inside these ranges and needn't reach their ends.
All inputs are finite; a program needn't handle non-finite values.
Results may differ from the reference program's by a relative error of at most 0.005.
Values may be sent and summed in bfloat16 or wider, within the bound.
A program may use at most 128 MiB of HBM per device.

```python
import math
import jax
import jax.numpy as jnp
from jax import lax

P_SIZE = 2048
NT = 512
F = 64
S = 512
C = 32
STEPS = 2


def with_spikes(result, key, source, target, blocks, factor):
    def block_of(dim):
        return (jnp.arange(result.shape[dim]) // (result.shape[dim] // blocks)).reshape((-1,) + (1,) * (result.ndim - 1 - dim))

    near = jax.random.permutation(key, blocks)[block_of(target)]
    other_side = (block_of(target) + blocks // 2) % blocks
    return jnp.where((block_of(source) == near) | (block_of(source) == other_side), factor * result, result)


def levels(stream_key, extent, split, smallest, largest):
    level, own = 1.0, jax.random.fold_in(stream_key, 6)
    for dim, parts in split:
        steps = jnp.exp(jax.random.uniform(jax.random.fold_in(own, dim), (parts,), jnp.float32, smallest / len(split), largest / len(split)))
        level = level * jnp.repeat(steps, extent[dim] // parts).reshape([-1 if axis == dim else 1 for axis in range(len(extent))])
    return level


def scatter_about(stream_key, dims, scale, limit, shards=(), kind=jnp.bfloat16):
    result = scale * jax.random.normal(stream_key, dims, jnp.float32)
    if shards:
        result = result * levels(stream_key, dims, shards, -0.22, 0.18)
    return jnp.clip(result, -limit, limit).astype(kind)


def heavy_noise(rng, shape, scale, most, shards, heavy, kind=jnp.bfloat16):
    entries = scale * jax.random.normal(rng, shape, jnp.float32)
    if shards:
        entries = entries * levels(rng, shape, shards, -0.22, 0.18)
    return jnp.clip(with_spikes(entries, jax.random.fold_in(rng, 3), *heavy), -most, most).astype(kind)


def setup_inputs(seed: int = 0) -> dict:
    seeds = jax.random.split(jax.random.key(seed), 8)
    return {
        "chain_state": scatter_about(seeds[0], (C, P_SIZE, NT), 1.0, 6.0, ((0, 4), (1, 8)), jnp.float32),
        "second_moment": jnp.clip(jnp.exp(math.log(2.0) - 2.0794415 * jax.random.uniform(seeds[1], (C, P_SIZE, NT), jnp.float32) ** levels(seeds[1], (C, P_SIZE, NT), ((0, 4), (1, 8)), -0.2, 0.2)), 0.25, 2.0),
        "noise": scatter_about(seeds[2], (STEPS, C, P_SIZE, NT), 1.0, 6.0, ((1, 4), (2, 8)), jnp.float32),
        "green": heavy_noise(seeds[3], (2, F, P_SIZE, S), (2 * P_SIZE) ** -0.5, 0.125, ((1, 4), (2, 8)), (2, 3, 8, 2.0)),
        "observed": scatter_about(seeds[4], (F, 2 * S), 1.0, 6.0, ((0, 4),), jnp.float32),
        "inv_noise": jnp.clip(jnp.exp(math.log(3.0) - 2.3025851 * jax.random.uniform(seeds[5], (F, S), jnp.float32) ** levels(seeds[5], (F, S), ((0, 4),), -0.2, 0.2)), 0.3, 3.0),
        "temper": jnp.clip(jnp.exp(math.log(1.0) - 1.609438 * jax.random.uniform(seeds[6], (C,), jnp.float32) ** levels(seeds[6], (C,), ((0, 4),), -0.2, 0.2)), 0.2, 1.0),
    }


decay_rate = 0.9
step_length = 0.5

def spectral_table(time_len, freq_total):
    time_index = jnp.arange(time_len, dtype=jnp.int32)[:, None]
    wave_number = jnp.arange(freq_total, dtype=jnp.int32)[None, :] + 1
    phase_angle = (time_index * wave_number % time_len).astype(jnp.float32) * (2.0 * math.pi / time_len)
    columns_table = jnp.stack([jnp.cos(phase_angle), -jnp.sin(phase_angle)], axis=-1).reshape(time_len, 2 * freq_total)
    return (columns_table / math.sqrt(time_len)).astype(jnp.bfloat16)

def per_frequency(inputs):
    real_in, imag_in, green_re, green_im, target, weight_row = inputs
    data_re = jnp.dot(real_in, green_re, preferred_element_type=jnp.float32) - jnp.dot(imag_in, green_im, preferred_element_type=jnp.float32)
    data_im = jnp.dot(real_in, green_im, preferred_element_type=jnp.float32) + jnp.dot(imag_in, green_re, preferred_element_type=jnp.float32)
    resid_re = (weight_row[:S] * (data_re - target[:S])).astype(jnp.bfloat16)
    resid_im = (weight_row[S:] * (data_im - target[S:])).astype(jnp.bfloat16)
    back_re = jnp.dot(resid_re, green_re.T, preferred_element_type=jnp.float32) + jnp.dot(resid_im, green_im.T, preferred_element_type=jnp.float32)
    back_im = jnp.dot(resid_im, green_re.T, preferred_element_type=jnp.float32) - jnp.dot(resid_re, green_im.T, preferred_element_type=jnp.float32)
    return (back_re.astype(jnp.bfloat16), back_im.astype(jnp.bfloat16))

def reference(chain_state, second_moment, noise, green, observed, inv_noise, temper):
    forward_table = spectral_table(NT, F)
    current = chain_state
    moment = second_moment
    weights_full = jnp.concatenate([inv_noise, inv_noise], axis=1)
    for step_num in range(STEPS):
        low_state = current.astype(jnp.bfloat16)
        spectrum = jnp.dot(low_state.reshape(C * P_SIZE, NT), forward_table, preferred_element_type=jnp.float32)
        spectrum = spectrum.astype(jnp.bfloat16).reshape(C, P_SIZE, F, 2)
        real_part = spectrum[..., 0].transpose(2, 0, 1)
        imag_part = spectrum[..., 1].transpose(2, 0, 1)
        back_re, back_im = lax.map(per_frequency, (real_part, imag_part, green[0], green[1], observed, weights_full))
        adjoint = jnp.stack([back_re, back_im], axis=-1).transpose(1, 2, 0, 3).reshape(C * P_SIZE, 2 * F)
        gradient = jnp.dot(adjoint, forward_table.T, preferred_element_type=jnp.float32).reshape(C, P_SIZE, NT)
        drift_term = temper[:, None, None] * gradient + current
        moment = decay_rate * moment + (1.0 - decay_rate) * drift_term * drift_term
        precondition = lax.rsqrt(moment)
        current = current - step_length * precondition * drift_term + math.sqrt(2.0 * step_length) * jnp.sqrt(precondition) * noise[step_num]
    return (current, moment)
```

```python
import functools
import math

import jax
import jax.numpy as jnp
from jax import lax
from jax.experimental import pallas as pl
from jax.experimental.pallas import tpu as pltpu
from jax.sharding import PartitionSpec as P

decay_rate = 0.9
step_length = 0.5
MESH = pl.DeviceIdType.MESH
LANES = 128
CHUNK_FREQS = 1
CORE_LAG = 2
HOP_LAG = 3
GATHER_LAG = 2


def spectral_table(time_len, freq_total):
    time_index = jnp.arange(time_len, dtype=jnp.int32)[:, None]
    wave_number = jnp.arange(freq_total, dtype=jnp.int32)[None, :] + 1
    phase_angle = (time_index * wave_number % time_len).astype(jnp.float32) * (
        2.0 * math.pi / time_len
    )
    columns_table = jnp.stack([jnp.cos(phase_angle), -jnp.sin(phase_angle)], axis=-1).reshape(
        time_len, 2 * freq_total
    )
    return (columns_table / math.sqrt(time_len)).astype(jnp.bfloat16)


def steps_kernel(
    freq_count, param_count, chunk_freqs,
    table_ref, temper_ref, obs_ref, inv_ref, state_hbm, moment_hbm, noise_hbm, green_hbm,
    adj_all, state, moment, last_noise,
    obs_rows, inv_rows, green, noise, rows32, spec, field, acc, core_out, core_in,
    up_out, up_in, down_out, down_in, wtd, adj,
    state_sem, green_sem, moment_sem, noise_sem, spec_send, spec_recv,
    line_send, line_recv, adj_send, adj_recv,
):
    freq_me = lax.axis_index("freq")
    param_me = lax.axis_index("param")
    steps, freq_loc = field.shape[0], field.shape[1]
    rows, slab = field.shape[3], field.shape[4]
    chains_loc = rows // 2
    all_rows, half = acc.shape[1], acc.shape[2]
    sensors = 2 * half
    col_blocks = slab // LANES
    columns = table_ref.shape[0]
    chunks = freq_loc // chunk_freqs
    line = param_count // 2
    core = lax.rem(param_me, 2)
    chip = param_me // 2
    core_peer = param_me + 1 - 2 * core
    above, below = param_me + 2, param_me - 2
    has_above, has_below = chip < line - 1, chip > 0

    def freq_peer(d):
        return lax.rem(freq_me + d, freq_count)

    barrier = pltpu.get_barrier_semaphore()
    for d in range(1, freq_count):
        pl.semaphore_signal(barrier, inc=1, device_id={"freq": freq_peer(d)}, device_id_type=MESH)
    pl.semaphore_signal(barrier, inc=1, device_id={"param": core_peer}, device_id_type=MESH)

    @pl.when(has_above)
    def _():
        pl.semaphore_signal(barrier, inc=1, device_id={"param": above}, device_id_type=MESH)

    @pl.when(has_below)
    def _():
        pl.semaphore_signal(barrier, inc=1, device_id={"param": below}, device_id_type=MESH)

    def state_copy(c):
        return pltpu.make_async_copy(state_hbm.at[c], state.at[c], state_sem.at[c])

    def green_copy(f):
        return pltpu.make_async_copy(green_hbm.at[:, f], green.at[f], green_sem.at[f])

    def moment_copy():
        return pltpu.make_async_copy(moment_hbm, moment, moment_sem.at[0])

    def noise_copy(s):
        return pltpu.make_async_copy(noise_hbm.at[s], noise.at[s], noise_sem.at[s])

    def last_noise_copy():
        return pltpu.make_async_copy(noise_hbm.at[steps - 1], last_noise, noise_sem.at[steps - 1])

    def spec_copy(s, i, d):
        part = pl.ds(i * chunk_freqs, chunk_freqs)
        return pltpu.make_async_remote_copy(
            src_ref=spec.at[s, freq_peer(d), part],
            dst_ref=field.at[s, part, freq_me],
            send_sem=spec_send.at[s, d - 1, i],
            recv_sem=spec_recv.at[s, d - 1, i],
            device_id={"freq": freq_peer(d)},
            device_id_type=MESH,
        )

    def param_copy(k, s, i, src, dst, peer):
        part = pl.ds(i * chunk_freqs, chunk_freqs)
        return pltpu.make_async_remote_copy(
            src_ref=src.at[part],
            dst_ref=dst.at[part],
            send_sem=line_send.at[k, s, i],
            recv_sem=line_recv.at[k, s, i],
            device_id={"param": peer},
            device_id_type=MESH,
        )

    def core_reduce(s, i):
        return param_copy(0, s, i, core_out.at[s], core_in.at[s], core_peer)

    def core_gather(s, i):
        return param_copy(1, s, i, wtd.at[s, core], wtd.at[s, core], core_peer)

    def up_copy(s, i):
        return param_copy(2, s, i, up_out.at[s], up_in.at[s], above)

    def down_copy(s, i):
        return param_copy(3, s, i, down_out.at[s], down_in.at[s], below)

    def adj_copy(s, i, d):
        part = pl.ds(i * chunk_freqs, chunk_freqs)
        return pltpu.make_async_remote_copy(
            src_ref=adj.at[s, part, freq_peer(d)],
            dst_ref=adj_all.at[s, freq_me, part],
            send_sem=adj_send.at[s, d - 1, i],
            recv_sem=adj_recv.at[s, d - 1, i],
            device_id={"freq": freq_peer(d)},
            device_id_type=MESH,
        )

    def transform(c, low):
        dims = (((1,), (1,)), ((), ()))
        result = lax.dot_general(table_ref[...], low, dims, preferred_element_type=jnp.float32)
        for b in range(col_blocks):
            block = result[:, b * LANES : (b + 1) * LANES]
            rows32[b, pl.ds(c, columns, stride=chains_loc)] = block

    def send_spectrum(s):
        @pl.loop(0, chunks)
        def _(i):
            for g in range(chunk_freqs):
                f = i * chunk_freqs + g
                for d in range(freq_count):
                    first = pl.multiple_of((freq_peer(d) * freq_loc + f) * rows, rows)
                    pieces = [rows32[b, pl.ds(first, rows)] for b in range(col_blocks)]
                    tile = jnp.concatenate(pieces, axis=1).astype(jnp.bfloat16)
                    if d == 0:
                        field[s, f, freq_me] = tile
                    else:
                        spec[s, freq_peer(d), f] = tile
            for d in range(1, freq_count):
                spec_copy(s, i, d).start()

    @pl.loop(0, chains_loc)
    def _(c):
        state_copy(c).start()

    for f in range(freq_loc):
        first = pl.multiple_of(core * half, half)
        inv_rows[f] = inv_ref[f : f + 1, pl.ds(first, half)]
        for ri in range(2):
            first = pl.multiple_of(ri * sensors + core * half, half)
            obs_rows[f, ri : ri + 1] = obs_ref[f : f + 1, pl.ds(first, half)]

    @pl.loop(0, chains_loc)
    def _(c):
        state_copy(c).wait()
        transform(c, state[c].astype(jnp.bfloat16))

    @pl.loop(0, freq_loc)
    def _(f):
        green_copy(f).start()

    moment_copy().start()
    for s in range(steps - 1):
        noise_copy(s).start()
    last_noise_copy().start()

    met = has_above.astype(jnp.int32) + has_below.astype(jnp.int32)
    pl.semaphore_wait(barrier, freq_count + met)
    send_spectrum(0)

    def turned(x, sign):
        wide = x.astype(jnp.float32)
        pieces = []
        for j in range(freq_count):
            re = wide[j * rows : j * rows + chains_loc]
            im = wide[j * rows + chains_loc : (j + 1) * rows]
            pieces += [im, -re] if sign < 0 else [-im, re]
        return jnp.concatenate(pieces, axis=0).astype(jnp.bfloat16)

    def forward(s, i):
        @pl.when(s == 0)
        def _():
            for g in range(chunk_freqs):
                green_copy(i * chunk_freqs + g).wait()

        for d in range(1, freq_count):
            spec_copy(s, i, d).wait_recv()
        for g in range(chunk_freqs):
            f = i * chunk_freqs + g
            x = field[s, f].reshape(all_rows, slab)
            both = jnp.concatenate([x, turned(x, 1)], axis=1)
            weights = green[f].reshape(2 * slab, sensors)
            data = jnp.dot(both, weights, preferred_element_type=jnp.float32)
            low, high = data[:, :half], data[:, half:]
            acc[f] = jnp.where(core == 0, low, high)
            core_out[s, f] = jnp.where(core == 0, high, low).astype(jnp.bfloat16)
        core_reduce(s, i).start()

    def merge(s, i):
        core_reduce(s, i).wait_recv()
        part = pl.ds(i * chunk_freqs, chunk_freqs)
        total = acc[part] + core_in[s, part].astype(jnp.float32)
        acc[part] = total

        @pl.when(chip == 0)
        def _():
            up_out[s, part] = total.astype(jnp.bfloat16)
            up_copy(s, i).start()

        @pl.when(chip == line - 1)
        def _():
            down_out[s, part] = total.astype(jnp.bfloat16)
            down_copy(s, i).start()

    def pass_up(s, i):
        up_copy(s, i).wait_recv()
        part = pl.ds(i * chunk_freqs, chunk_freqs)
        total = acc[part] + up_in[s, part].astype(jnp.float32)
        up_out[s, part] = total.astype(jnp.bfloat16)
        up_copy(s, i).start()

    def pass_down(s, i):
        down_copy(s, i).wait_recv()
        part = pl.ds(i * chunk_freqs, chunk_freqs)
        total = acc[part] + down_in[s, part].astype(jnp.float32)
        down_out[s, part] = total.astype(jnp.bfloat16)
        down_copy(s, i).start()

    def weigh(s, i):
        part = pl.ds(i * chunk_freqs, chunk_freqs)

        @pl.when(chip == line - 1)
        def _():
            up_copy(s, i).wait_recv()

        @pl.when(chip == 0)
        def _():
            down_copy(s, i).wait_recv()

        @pl.when(has_below)
        def _():
            acc[part] = acc[part] + up_in[s, part].astype(jnp.float32)

        @pl.when(has_above)
        def _():
            acc[part] = acc[part] + down_in[s, part].astype(jnp.float32)

        for g in range(chunk_freqs):
            f = i * chunk_freqs + g
            total = acc[f]
            target = obs_rows[f]
            weight = inv_rows[f]
            pieces = []
            for j in range(freq_count):
                for ri in range(2):
                    here = j * rows + ri * chains_loc
                    apart = total[here : here + chains_loc] - target[ri : ri + 1]
                    pieces.append(weight * apart)
            wtd[s, core, f] = jnp.concatenate(pieces, axis=0).astype(jnp.bfloat16)
        core_gather(s, i).start()

    def backward(s, i):
        core_gather(s, i).wait_recv()
        dims = (((1,), (1,)), ((), ()))
        for g in range(chunk_freqs):
            f = i * chunk_freqs + g
            w = jnp.concatenate([wtd[s, 0, f], wtd[s, 1, f]], axis=1)
            first = lax.dot_general(w, green[f, 0], dims, preferred_element_type=jnp.float32)
            second = lax.dot_general(
                turned(w, -1), green[f, 1], dims, preferred_element_type=jnp.float32
            )
            back = (first + second).astype(jnp.bfloat16)
            adj[s, f] = back.reshape(freq_count, rows, slab)
            adj_all[s, freq_me, f] = adj[s, f, freq_me]
        for d in range(1, freq_count):
            adj_copy(s, i, d).start()

    up_depth, down_depth = chip, line - 1 - chip
    deepest = jnp.maximum(up_depth, down_depth)
    up_lag = CORE_LAG + HOP_LAG * up_depth
    down_lag = CORE_LAG + HOP_LAG * down_depth
    weigh_lag = CORE_LAG + HOP_LAG * deepest
    inside = has_above & has_below

    @pl.loop(0, steps)
    def _(s):
        @pl.loop(0, chunks + CORE_LAG + HOP_LAG * (line - 1) + GATHER_LAG)
        def _(tick):
            def stage(lag, work, allowed=None):
                due = (tick >= lag) & (tick < chunks + lag)

                @pl.when(due if allowed is None else due & allowed)
                def _():
                    work(s, tick - lag)

            stage(CORE_LAG, merge)
            stage(up_lag, pass_up, inside)
            stage(down_lag, pass_down, inside)
            stage(weigh_lag, weigh)
            stage(0, forward)
            stage(weigh_lag + GATHER_LAG, backward)

        @pl.loop(0, chunks)
        def _(i):
            for d in range(1, freq_count):
                adj_copy(s, i, d).wait_recv()

        @pl.when(s < steps - 1)
        def _():
            @pl.when(s == 0)
            def _():
                moment_copy().wait()

            noise_copy(s).wait()

            @pl.loop(0, freq_count)
            def _(j):
                for f in range(freq_loc):
                    first = pl.multiple_of((j * freq_loc + f) * rows, rows)
                    tile = adj_all[s, j, f].astype(jnp.float32)
                    for b in range(col_blocks):
                        block = tile[:, b * LANES : (b + 1) * LANES]
                        rows32[b, pl.ds(first, rows)] = block

            @pl.loop(0, chains_loc)
            def _(c):
                current, spread = advance(
                    c, rows32, table_ref, temper_ref, state[c], moment[c], noise[s, c]
                )
                state[c] = current
                moment[c] = spread
                transform(c, current.astype(jnp.bfloat16))

            send_spectrum(s + 1)

    last_noise_copy().wait()

    @pl.loop(0, steps)
    def _(s):
        @pl.loop(0, chunks)
        def _(i):
            for d in range(1, freq_count):
                spec_copy(s, i, d).wait_send()
                adj_copy(s, i, d).wait_send()
            core_reduce(s, i).wait_send()
            core_gather(s, i).wait_send()

            @pl.when(has_above)
            def _():
                up_copy(s, i).wait_send()

            @pl.when(has_below)
            def _():
                down_copy(s, i).wait_send()


def advance(c, rows32, table_ref, temper_ref, current, spread, push):
    columns, chains_loc = table_ref.shape[0], rows32.shape[1] // table_ref.shape[0]
    pieces = [
        rows32[b, pl.ds(c, columns, stride=chains_loc)] for b in range(rows32.shape[0])
    ]
    mine = jnp.concatenate(pieces, axis=1).astype(jnp.bfloat16)
    gradient = lax.dot_general(
        mine, table_ref[...], (((0,), (0,)), ((), ())), preferred_element_type=jnp.float32
    )
    drift_term = temper_ref[c] * gradient + current
    spread = decay_rate * spread + (1.0 - decay_rate) * drift_term * drift_term
    precondition = lax.rsqrt(spread)
    root = precondition * lax.rsqrt(precondition)
    current = (
        current
        - step_length * precondition * drift_term
        + math.sqrt(2.0 * step_length) * root * push
    )
    return current, spread


def final_kernel(
    table_ref, temper_ref, adj_all, state, moment, push, state_hbm, moment_hbm,
    rows32, new_state, new_moment, state_sem, moment_sem,
):
    last = adj_all.shape[0] - 1
    freq_count, freq_loc, rows, slab = adj_all.shape[1:]

    def state_copy(c):
        return pltpu.make_async_copy(new_state.at[c], state_hbm.at[c], state_sem.at[c])

    def moment_copy(c):
        return pltpu.make_async_copy(new_moment.at[c], moment_hbm.at[c], moment_sem.at[c])

    @pl.loop(0, freq_count)
    def _(j):
        for f in range(freq_loc):
            first = pl.multiple_of((j * freq_loc + f) * rows, rows)
            tile = adj_all[last, j, f].astype(jnp.float32)
            for b in range(slab // LANES):
                rows32[b, pl.ds(first, rows)] = tile[:, b * LANES : (b + 1) * LANES]

    @pl.loop(0, state.shape[0])
    def _(c):
        current, spread = advance(
            c, rows32, table_ref, temper_ref, state[c], moment[c], push[c]
        )
        new_state[c] = current
        new_moment[c] = spread
        state_copy(c).start()
        moment_copy(c).start()

    @pl.loop(0, state.shape[0])
    def _(c):
        state_copy(c).wait()
        moment_copy(c).wait()


def fits_kernel(chain_shape, green_shape):
    chains_loc, slab = chain_shape[0], chain_shape[1]
    param_count = lax.axis_size("param")
    return (
        chains_loc % 8 == 0
        and slab % LANES == 0
        and chain_shape[2] % LANES == 0
        and green_shape[3] % (2 * LANES) == 0
        and green_shape[1] % CHUNK_FREQS == 0
        and param_count == 8
        and lax.axis_size("freq") > 1
    )


def kernel_steps(chain_state, second_moment, noise, green, observed, inv_noise, temper):
    chains_loc, slab, time_len = chain_state.shape
    freq_loc, sensors = green.shape[1], green.shape[3]
    steps = noise.shape[0]
    freq_count, param_count = lax.axis_size("freq"), lax.axis_size("param")
    columns = 2 * freq_loc * freq_count
    table = spectral_table(time_len, freq_loc * freq_count).T
    chunks = freq_loc // CHUNK_FREQS
    rows, half = 2 * chains_loc, sensors // 2
    all_rows = freq_count * rows
    bf16, f32 = jnp.bfloat16, jnp.float32
    dma = pltpu.SemaphoreType.DMA
    vmem = pl.BlockSpec(memory_space=pltpu.VMEM)
    smem = pl.BlockSpec(memory_space=pltpu.SMEM)
    hbm = pl.BlockSpec(memory_space=pltpu.HBM)
    line_buf = pltpu.VMEM((steps, freq_loc, all_rows, half), bf16)
    rows32 = pltpu.VMEM((slab // LANES, columns * chains_loc, LANES), f32)
    peers = freq_count - 1
    adj_all, state, moment, push = pl.pallas_call(
        functools.partial(steps_kernel, freq_count, param_count, CHUNK_FREQS),
        out_shape=[
            jax.ShapeDtypeStruct((steps, freq_count, freq_loc, rows, slab), bf16),
            jax.ShapeDtypeStruct(chain_state.shape, f32),
            jax.ShapeDtypeStruct(chain_state.shape, f32),
            jax.ShapeDtypeStruct(chain_state.shape, f32),
        ],
        in_specs=[vmem, smem, vmem, vmem, hbm, hbm, hbm, hbm],
        out_specs=[vmem, vmem, vmem, vmem],
        scratch_shapes=[
            pltpu.VMEM((freq_loc, 2, half), f32),
            pltpu.VMEM((freq_loc, 1, half), f32),
            pltpu.VMEM((freq_loc, 2, slab, sensors), bf16),
            pltpu.VMEM((max(steps - 1, 1),) + chain_state.shape, f32),
            rows32,
            pltpu.VMEM((steps, freq_count, freq_loc, rows, slab), bf16),
            pltpu.VMEM((steps, freq_loc, freq_count, rows, slab), bf16),
            pltpu.VMEM((freq_loc, all_rows, half), f32),
            line_buf, line_buf, line_buf, line_buf, line_buf, line_buf,
            pltpu.VMEM((steps, 2, freq_loc, all_rows, half), bf16),
            pltpu.VMEM((steps, freq_loc, freq_count, rows, slab), bf16),
            dma((chains_loc,)),
            dma((freq_loc,)),
            dma((1,)),
            dma((steps,)),
            dma((steps, peers, chunks)),
            dma((steps, peers, chunks)),
            dma((4, steps, chunks)),
            dma((4, steps, chunks)),
            dma((steps, peers, chunks)),
            dma((steps, peers, chunks)),
        ],
        compiler_params=pltpu.CompilerParams(
            collective_id=0, has_side_effects=True, vmem_limit_bytes=44 * 2**20
        ),
    )(table, temper, observed, inv_noise, chain_state, second_moment, noise, green)
    return pl.pallas_call(
        final_kernel,
        out_shape=[
            jax.ShapeDtypeStruct(chain_state.shape, f32),
            jax.ShapeDtypeStruct(chain_state.shape, f32),
        ],
        in_specs=[vmem, smem, vmem, vmem, vmem, vmem],
        out_specs=[hbm, hbm],
        scratch_shapes=[
            rows32,
            pltpu.VMEM(chain_state.shape, f32),
            pltpu.VMEM(chain_state.shape, f32),
            dma((chains_loc,)),
            dma((chains_loc,)),
        ],
        compiler_params=pltpu.CompilerParams(vmem_limit_bytes=14 * 2**20),
    )(table, temper, adj_all, state, moment, push)


def on_device(chain_state, second_moment, noise, green, observed, inv_noise, temper):
    if fits_kernel(chain_state.shape, green.shape):
        return kernel_steps(
            chain_state, second_moment, noise, green, observed, inv_noise, temper
        )
    chains_loc, slab_rows, time_len = chain_state.shape
    freq_loc = green.shape[1]
    freq_count = lax.axis_size("freq")
    freq_total = freq_loc * freq_count
    chains = chains_loc * freq_count
    forward_table = spectral_table(time_len, freq_total)
    inverse_table = forward_table.T
    green_re = green[0]
    green_im = green[1]
    upper_rows = jnp.concatenate([green_re, green_im], axis=2)
    lower_rows = jnp.concatenate([-green_im, green_re], axis=2)
    kernel = jnp.concatenate([upper_rows, lower_rows], axis=1)
    weights = jnp.concatenate([inv_noise, inv_noise], axis=1)
    temper_cols = temper[:, None, None]
    current = chain_state
    moment = second_moment
    for step_num in range(noise.shape[0]):
        low_state = current.astype(jnp.bfloat16)
        local_spec = jnp.dot(
            low_state.reshape(chains_loc * slab_rows, time_len),
            forward_table,
            preferred_element_type=jnp.float32,
        )
        local_spec = local_spec.astype(jnp.bfloat16).reshape(chains_loc, slab_rows, 2 * freq_total)
        spectrum = lax.all_to_all(local_spec, "freq", split_axis=2, concat_axis=0, tiled=True)
        mixed_spec = (
            spectrum.reshape(chains, slab_rows, freq_loc, 2)
            .transpose(2, 0, 3, 1)
            .reshape(freq_loc, chains, 2 * slab_rows)
        )
        partial_data = jnp.einsum(
            "fcq,fqs->fcs", mixed_spec, kernel, preferred_element_type=jnp.float32
        )
        predicted = lax.psum(partial_data.astype(jnp.bfloat16), "param").astype(jnp.float32)
        weighted = (weights[:, None, :] * (predicted - observed[:, None, :])).astype(jnp.bfloat16)
        adjoint = jnp.einsum(
            "fcs,fqs->fcq", weighted, kernel, preferred_element_type=jnp.float32
        ).astype(jnp.bfloat16)
        adjoint = (
            adjoint.reshape(freq_loc, chains, 2, slab_rows)
            .transpose(1, 3, 0, 2)
            .reshape(chains, slab_rows, 2 * freq_loc)
        )
        own_adjoint = lax.all_to_all(adjoint, "freq", split_axis=0, concat_axis=2, tiled=True)
        gradient = jnp.dot(
            own_adjoint.reshape(chains_loc * slab_rows, 2 * freq_total),
            inverse_table,
            preferred_element_type=jnp.float32,
        )
        gradient = gradient.reshape(chains_loc, slab_rows, time_len)
        drift_term = temper_cols * gradient + current
        moment = decay_rate * moment + (1.0 - decay_rate) * drift_term * drift_term
        precondition = lax.rsqrt(moment)
        current = (
            current
            - step_length * precondition * drift_term
            + math.sqrt(2.0 * step_length) * jnp.sqrt(precondition) * noise[step_num]
        )
    return (current, moment)


def solution(mesh):
    return jax.shard_map(
        on_device,
        mesh=mesh,
        in_specs=(
            P("freq", "param", None),
            P("freq", "param", None),
            P(None, "freq", "param", None),
            P(None, "freq", "param", None),
            P("freq", None),
            P("freq", None),
            P("freq"),
        ),
        out_specs=(P("freq", "param", None), P("freq", "param", None)),
        check_vma=False,
    )
```

```python
import functools
import math

import jax
import jax.numpy as jnp
from jax import lax
from jax.experimental import pallas as pl
from jax.experimental.pallas import tpu as pltpu
from jax.sharding import PartitionSpec as P

decay_rate = 0.9
step_length = 0.5
MESH = pl.DeviceIdType.MESH
LANES = 128
CHUNK_FREQS = 1
CORE_LAG = 3
HOP_LAG = 5
GATHER_LAG = 4


def spectral_table(time_len, freq_total):
    time_index = jnp.arange(time_len, dtype=jnp.int32)[:, None]
    wave_number = jnp.arange(freq_total, dtype=jnp.int32)[None, :] + 1
    phase_angle = (time_index * wave_number % time_len).astype(jnp.float32) * (
        2.0 * math.pi / time_len
    )
    columns_table = jnp.stack([jnp.cos(phase_angle), -jnp.sin(phase_angle)], axis=-1).reshape(
        time_len, 2 * freq_total
    )
    return (columns_table / math.sqrt(time_len)).astype(jnp.bfloat16)


def steps_kernel(
    freq_count, param_count, chunk_freqs,
    table_ref, temper_hbm, obs_hbm, inv_hbm, state_hbm, moment_hbm, noise_hbm, green_hbm,
    adj_all, state, moment,
    temper_ref, obs_all, inv_all, obs_rows, inv_rows, green, noise, rows32, spec, field, acc, core_out, core_in,
    up_out, up_in, down_out, down_in, wtd, adj,
    small_sem, state_sem, green_sem, moment_sem, noise_sem, spec_send, spec_recv,
    line_send, line_recv, adj_send, adj_recv,
):
    freq_me = lax.axis_index("freq")
    param_me = lax.axis_index("param")
    steps, freq_loc = field.shape[0], field.shape[1]
    rows, slab = field.shape[3], field.shape[4]
    chains_loc = rows // 2
    all_rows, half = acc.shape[1], acc.shape[2]
    sensors = 2 * half
    col_blocks = slab // LANES
    columns = table_ref.shape[0]
    chunks = freq_loc // chunk_freqs
    line = param_count // 2
    core = lax.rem(param_me, 2)
    chip = param_me // 2
    core_peer = param_me + 1 - 2 * core
    above, below = param_me + 2, param_me - 2
    has_above, has_below = chip < line - 1, chip > 0

    def freq_peer(d):
        return lax.rem(freq_me + d, freq_count)

    barrier = pltpu.get_barrier_semaphore()
    for d in range(1, freq_count):
        pl.semaphore_signal(barrier, inc=1, device_id={"freq": freq_peer(d)}, device_id_type=MESH)
    pl.semaphore_signal(barrier, inc=1, device_id={"param": core_peer}, device_id_type=MESH)

    @pl.when(has_above)
    def _():
        pl.semaphore_signal(barrier, inc=1, device_id={"param": above}, device_id_type=MESH)

    @pl.when(has_below)
    def _():
        pl.semaphore_signal(barrier, inc=1, device_id={"param": below}, device_id_type=MESH)

    def state_copy(c):
        return pltpu.make_async_copy(state_hbm.at[c], state.at[c], state_sem.at[c])

    def green_copy(f):
        return pltpu.make_async_copy(green_hbm.at[:, f], green.at[f], green_sem.at[f])

    def moment_copy(c):
        return pltpu.make_async_copy(moment_hbm.at[c], moment.at[c], moment_sem.at[0])

    def noise_copy(s, c):
        return pltpu.make_async_copy(noise_hbm.at[s, c], noise.at[s, c], noise_sem.at[s])

    def obs_copy():
        return pltpu.make_async_copy(obs_hbm, obs_all, small_sem.at[0])

    def temper_copy():
        return pltpu.make_async_copy(temper_hbm, temper_ref, small_sem.at[2])

    def inv_copy():
        return pltpu.make_async_copy(inv_hbm, inv_all, small_sem.at[1])

    def spec_copy(s, i, d):
        part = pl.ds(i * chunk_freqs, chunk_freqs)
        return pltpu.make_async_remote_copy(
            src_ref=spec.at[s, freq_peer(d), part],
            dst_ref=field.at[s, part, freq_me],
            send_sem=spec_send.at[0],
            recv_sem=spec_recv.at[i],
            device_id={"freq": freq_peer(d)},
            device_id_type=MESH,
        )

    def param_copy(k, s, i, src, dst, peer):
        part = pl.ds(i * chunk_freqs, chunk_freqs)
        return pltpu.make_async_remote_copy(
            src_ref=src.at[part],
            dst_ref=dst.at[part],
            send_sem=line_send.at[k],
            recv_sem=line_recv.at[k, i],
            device_id={"param": peer},
            device_id_type=MESH,
        )

    def spec_arrival(s, i):
        here = field.at[s, pl.ds(i * chunk_freqs, chunk_freqs), pl.ds(0, freq_count - 1)]
        return pltpu.make_async_copy(here, here, spec_recv.at[i])

    def spec_departure(s):
        here = spec.at[s, pl.ds(0, freq_count - 1)]
        return pltpu.make_async_copy(here, here, spec_send.at[0])

    def adj_arrival(s):
        here = adj_all.at[s, pl.ds(0, freq_count - 1)]
        return pltpu.make_async_copy(here, here, adj_recv.at[0])

    def adj_departure(s):
        here = adj.at[s, :, pl.ds(0, freq_count - 1)]
        return pltpu.make_async_copy(here, here, adj_send.at[0])

    def line_departure(k, s):
        here = core_out.at[s]
        return pltpu.make_async_copy(here, here, line_send.at[k])

    def core_reduce(s, i):
        return param_copy(0, s, i, core_out.at[s], core_in.at[s], core_peer)

    def core_gather(s, i):
        return param_copy(1, s, i, wtd.at[s, core], wtd.at[s, core], core_peer)

    def up_copy(s, i):
        return param_copy(2, s, i, up_out.at[s], up_in.at[s], above)

    def down_copy(s, i):
        return param_copy(3, s, i, down_out.at[s], down_in.at[s], below)

    def adj_copy(s, i, d):
        part = pl.ds(i * chunk_freqs, chunk_freqs)
        return pltpu.make_async_remote_copy(
            src_ref=adj.at[s, part, freq_peer(d)],
            dst_ref=adj_all.at[s, freq_me, part],
            send_sem=adj_send.at[0],
            recv_sem=adj_recv.at[0],
            device_id={"freq": freq_peer(d)},
            device_id_type=MESH,
        )

    def transform(c, low):
        dims = (((1,), (1,)), ((), ()))
        result = lax.dot_general(table_ref[...], low, dims, preferred_element_type=jnp.float32)
        for b in range(col_blocks):
            block = result[:, b * LANES : (b + 1) * LANES]
            rows32[b, pl.ds(c, columns, stride=chains_loc)] = block

    def send_spectrum(s):
        @pl.loop(0, chunks)
        def _(i):
            for g in range(chunk_freqs):
                f = i * chunk_freqs + g
                for d in range(freq_count):
                    first = pl.multiple_of((freq_peer(d) * freq_loc + f) * rows, rows)
                    pieces = [rows32[b, pl.ds(first, rows)] for b in range(col_blocks)]
                    tile = jnp.concatenate(pieces, axis=1).astype(jnp.bfloat16)
                    if d == 0:
                        field[s, f, freq_me] = tile
                    else:
                        spec[s, freq_peer(d), f] = tile
            for d in range(1, freq_count):
                spec_copy(s, i, d).start()

    @pl.loop(0, chains_loc)
    def _(c):
        state_copy(c).start()

    obs_copy().start()
    inv_copy().start()
    temper_copy().start()

    @pl.loop(0, chains_loc)
    def _(c):
        state_copy(c).wait()
        transform(c, state[c].astype(jnp.bfloat16))

    @pl.loop(0, freq_loc)
    def _(f):
        green_copy(f).start()

    @pl.loop(0, chains_loc)
    def _(c):
        moment_copy(c).start()
        for s in range(steps - 1):
            noise_copy(s, c).start()

    met = has_above.astype(jnp.int32) + has_below.astype(jnp.int32)
    pl.semaphore_wait(barrier, freq_count + met)
    send_spectrum(0)
    obs_copy().wait()
    inv_copy().wait()
    temper_copy().wait()
    for f in range(freq_loc):
        first = pl.multiple_of(core * half, half)
        inv_rows[f] = inv_all[f : f + 1, pl.ds(first, half)]
        for ri in range(2):
            first = pl.multiple_of(ri * sensors + core * half, half)
            obs_rows[f, ri : ri + 1] = obs_all[f : f + 1, pl.ds(first, half)]

    def turned(x, sign):
        wide = x.astype(jnp.float32)
        pieces = []
        for j in range(freq_count):
            re = wide[j * rows : j * rows + chains_loc]
            im = wide[j * rows + chains_loc : (j + 1) * rows]
            pieces += [im, -re] if sign < 0 else [-im, re]
        return jnp.concatenate(pieces, axis=0).astype(jnp.bfloat16)

    def forward(s, i):
        @pl.when(s == 0)
        def _():
            for g in range(chunk_freqs):
                green_copy(i * chunk_freqs + g).wait()

        spec_arrival(s, i).wait()
        for g in range(chunk_freqs):
            f = i * chunk_freqs + g
            x = field[s, f].reshape(all_rows, slab)
            both = jnp.concatenate([x, turned(x, 1)], axis=1)
            weights = green[f].reshape(2 * slab, sensors)
            data = jnp.dot(both, weights, preferred_element_type=jnp.float32)
            low, high = data[:, :half], data[:, half:]
            acc[f] = jnp.where(core == 0, low, high)
            core_out[s, f] = jnp.where(core == 0, high, low).astype(jnp.bfloat16)
        core_reduce(s, i).start()

    def merge(s, i):
        core_reduce(s, i).wait_recv()
        part = pl.ds(i * chunk_freqs, chunk_freqs)
        total = acc[part] + core_in[s, part].astype(jnp.float32)
        acc[part] = total

        @pl.when(chip == 0)
        def _():
            up_out[s, part] = total.astype(jnp.bfloat16)
            up_copy(s, i).start()

        @pl.when(chip == line - 1)
        def _():
            down_out[s, part] = total.astype(jnp.bfloat16)
            down_copy(s, i).start()

    def pass_up(s, i):
        up_copy(s, i).wait_recv()
        part = pl.ds(i * chunk_freqs, chunk_freqs)
        total = acc[part] + up_in[s, part].astype(jnp.float32)
        up_out[s, part] = total.astype(jnp.bfloat16)
        up_copy(s, i).start()

    def pass_down(s, i):
        down_copy(s, i).wait_recv()
        part = pl.ds(i * chunk_freqs, chunk_freqs)
        total = acc[part] + down_in[s, part].astype(jnp.float32)
        down_out[s, part] = total.astype(jnp.bfloat16)
        down_copy(s, i).start()

    def weigh(s, i):
        part = pl.ds(i * chunk_freqs, chunk_freqs)

        @pl.when(chip == line - 1)
        def _():
            up_copy(s, i).wait_recv()

        @pl.when(chip == 0)
        def _():
            down_copy(s, i).wait_recv()

        @pl.when(has_below)
        def _():
            acc[part] = acc[part] + up_in[s, part].astype(jnp.float32)

        @pl.when(has_above)
        def _():
            acc[part] = acc[part] + down_in[s, part].astype(jnp.float32)

        for g in range(chunk_freqs):
            f = i * chunk_freqs + g
            total = acc[f]
            target = obs_rows[f]
            weight = inv_rows[f]
            pieces = []
            for j in range(freq_count):
                for ri in range(2):
                    here = j * rows + ri * chains_loc
                    apart = total[here : here + chains_loc] - target[ri : ri + 1]
                    pieces.append(weight * apart)
            wtd[s, core, f] = jnp.concatenate(pieces, axis=0).astype(jnp.bfloat16)
        core_gather(s, i).start()

    def backward(s, i):
        core_gather(s, i).wait_recv()
        dims = (((1,), (1,)), ((), ()))
        for g in range(chunk_freqs):
            f = i * chunk_freqs + g
            w = jnp.concatenate([wtd[s, 0, f], wtd[s, 1, f]], axis=1)
            first = lax.dot_general(w, green[f, 0], dims, preferred_element_type=jnp.float32)
            second = lax.dot_general(
                turned(w, -1), green[f, 1], dims, preferred_element_type=jnp.float32
            )
            back = (first + second).astype(jnp.bfloat16)
            adj[s, f] = back.reshape(freq_count, rows, slab)
            adj_all[s, freq_me, f] = adj[s, f, freq_me]
        for d in range(1, freq_count):
            adj_copy(s, i, d).start()

    up_depth, down_depth = chip, line - 1 - chip
    deepest = jnp.maximum(up_depth, down_depth)
    up_lag = CORE_LAG + HOP_LAG * up_depth
    down_lag = CORE_LAG + HOP_LAG * down_depth
    weigh_lag = CORE_LAG + HOP_LAG * deepest
    inside = has_above & has_below

    @pl.loop(0, steps)
    def _(s):
        @pl.loop(0, chunks + CORE_LAG + HOP_LAG * (line - 1) + GATHER_LAG)
        def _(tick):
            def stage(lag, work, allowed=None):
                due = (tick >= lag) & (tick < chunks + lag)

                @pl.when(due if allowed is None else due & allowed)
                def _():
                    work(s, tick - lag)

            stage(CORE_LAG, merge)
            stage(up_lag, pass_up, inside)
            stage(down_lag, pass_down, inside)
            stage(weigh_lag, weigh)
            stage(0, forward)
            stage(weigh_lag + GATHER_LAG, backward)

        adj_arrival(s).wait()
        spec_departure(s).wait()
        adj_departure(s).wait()
        for k in range(2):
            line_departure(k, s).wait()

        @pl.when(has_above)
        def _():
            line_departure(2, s).wait()

        @pl.when(has_below)
        def _():
            line_departure(3, s).wait()

        @pl.when(s < steps - 1)
        def _():
            @pl.when(s == 0)
            def _():
                pltpu.make_async_copy(moment, moment, moment_sem.at[0]).wait()

            pltpu.make_async_copy(noise.at[s], noise.at[s], noise_sem.at[s]).wait()

            @pl.loop(0, freq_count)
            def _(j):
                for f in range(freq_loc):
                    first = pl.multiple_of((j * freq_loc + f) * rows, rows)
                    tile = adj_all[s, j, f].astype(jnp.float32)
                    for b in range(col_blocks):
                        block = tile[:, b * LANES : (b + 1) * LANES]
                        rows32[b, pl.ds(first, rows)] = block

            @pl.loop(0, chains_loc)
            def _(c):
                current, spread = advance(
                    c, rows32, table_ref, temper_ref, state[c], moment[c], noise[s, c]
                )
                state[c] = current
                moment[c] = spread
                transform(c, current.astype(jnp.bfloat16))

            send_spectrum(s + 1)


def advance(c, rows32, table_ref, temper_ref, current, spread, push):
    columns, chains_loc = table_ref.shape[0], rows32.shape[1] // table_ref.shape[0]
    pieces = [
        rows32[b, pl.ds(c, columns, stride=chains_loc)] for b in range(rows32.shape[0])
    ]
    mine = jnp.concatenate(pieces, axis=1).astype(jnp.bfloat16)
    gradient = lax.dot_general(
        mine, table_ref[...], (((0,), (0,)), ((), ())), preferred_element_type=jnp.float32
    )
    drift_term = temper_ref[c] * gradient + current
    spread = decay_rate * spread + (1.0 - decay_rate) * drift_term * drift_term
    precondition = lax.rsqrt(spread)
    root = precondition * lax.rsqrt(precondition)
    current = (
        current
        - step_length * precondition * drift_term
        + math.sqrt(2.0 * step_length) * root * push
    )
    return current, spread


def final_kernel(
    table_ref, temper_ref, adj_all, state, moment, noise_hbm, state_hbm, moment_hbm,
    rows32, push, new_state, new_moment, push_sem, state_sem, moment_sem,
):
    last = adj_all.shape[0] - 1
    freq_count, freq_loc, rows, slab = adj_all.shape[1:]

    def state_copy(c):
        return pltpu.make_async_copy(new_state.at[c], state_hbm.at[c], state_sem.at[c])

    def moment_copy(c):
        return pltpu.make_async_copy(new_moment.at[c], moment_hbm.at[c], moment_sem.at[c])

    def push_copy(c):
        return pltpu.make_async_copy(noise_hbm.at[last, c], push.at[c], push_sem.at[c])

    @pl.loop(0, state.shape[0])
    def _(c):
        push_copy(c).start()

    @pl.loop(0, freq_count)
    def _(j):
        for f in range(freq_loc):
            first = pl.multiple_of((j * freq_loc + f) * rows, rows)
            tile = adj_all[last, j, f].astype(jnp.float32)
            for b in range(slab // LANES):
                rows32[b, pl.ds(first, rows)] = tile[:, b * LANES : (b + 1) * LANES]

    @pl.loop(0, state.shape[0])
    def _(c):
        push_copy(c).wait()
        current, spread = advance(
            c, rows32, table_ref, temper_ref, state[c], moment[c], push[c]
        )
        new_state[c] = current
        new_moment[c] = spread
        state_copy(c).start()
        moment_copy(c).start()

    @pl.loop(0, state.shape[0])
    def _(c):
        state_copy(c).wait()
        moment_copy(c).wait()


def fits_kernel(chain_shape, green_shape):
    chains_loc, slab = chain_shape[0], chain_shape[1]
    param_count = lax.axis_size("param")
    return (
        chains_loc % 8 == 0
        and slab % LANES == 0
        and chain_shape[2] % LANES == 0
        and green_shape[3] % (2 * LANES) == 0
        and green_shape[1] % CHUNK_FREQS == 0
        and param_count == 8
        and lax.axis_size("freq") > 1
    )


def kernel_steps(chain_state, second_moment, noise, green, observed, inv_noise, temper):
    chains_loc, slab, time_len = chain_state.shape
    freq_loc, sensors = green.shape[1], green.shape[3]
    steps = noise.shape[0]
    freq_count, param_count = lax.axis_size("freq"), lax.axis_size("param")
    columns = 2 * freq_loc * freq_count
    table = spectral_table(time_len, freq_loc * freq_count).T
    chunks = freq_loc // CHUNK_FREQS
    rows, half = 2 * chains_loc, sensors // 2
    all_rows = freq_count * rows
    bf16, f32 = jnp.bfloat16, jnp.float32
    dma = pltpu.SemaphoreType.DMA
    vmem = pl.BlockSpec(memory_space=pltpu.VMEM)
    smem = pl.BlockSpec(memory_space=pltpu.SMEM)
    hbm = pl.BlockSpec(memory_space=pltpu.HBM)
    line_buf = pltpu.VMEM((steps, freq_loc, all_rows, half), bf16)
    rows32 = pltpu.VMEM((slab // LANES, columns * chains_loc, LANES), f32)
    adj_all, state, moment = pl.pallas_call(
        functools.partial(steps_kernel, freq_count, param_count, CHUNK_FREQS),
        out_shape=[
            jax.ShapeDtypeStruct((steps, freq_count, freq_loc, rows, slab), bf16),
            jax.ShapeDtypeStruct(chain_state.shape, f32),
            jax.ShapeDtypeStruct(chain_state.shape, f32),
        ],
        in_specs=[vmem, hbm, hbm, hbm, hbm, hbm, hbm, hbm],
        out_specs=[vmem, vmem, vmem],
        scratch_shapes=[
            pltpu.SMEM(temper.shape, f32),
            pltpu.VMEM(observed.shape, f32),
            pltpu.VMEM(inv_noise.shape, f32),
            pltpu.VMEM((freq_loc, 2, half), f32),
            pltpu.VMEM((freq_loc, 1, half), f32),
            pltpu.VMEM((freq_loc, 2, slab, sensors), bf16),
            pltpu.VMEM((max(steps - 1, 1),) + chain_state.shape, f32),
            rows32,
            pltpu.VMEM((steps, freq_count, freq_loc, rows, slab), bf16),
            pltpu.VMEM((steps, freq_loc, freq_count, rows, slab), bf16),
            pltpu.VMEM((freq_loc, all_rows, half), f32),
            line_buf, line_buf, line_buf, line_buf, line_buf, line_buf,
            pltpu.VMEM((steps, 2, freq_loc, all_rows, half), bf16),
            pltpu.VMEM((steps, freq_loc, freq_count, rows, slab), bf16),
            dma((3,)),
            dma((chains_loc,)),
            dma((freq_loc,)),
            dma((1,)),
            dma((max(steps - 1, 1),)),
            dma((1,)),
            dma((chunks,)),
            dma((4,)),
            dma((4, chunks)),
            dma((1,)),
            dma((1,)),
        ],
        compiler_params=pltpu.CompilerParams(
            collective_id=0, has_side_effects=True, vmem_limit_bytes=44 * 2**20
        ),
    )(table, temper, observed, inv_noise, chain_state, second_moment, noise, green)
    return pl.pallas_call(
        final_kernel,
        out_shape=[
            jax.ShapeDtypeStruct(chain_state.shape, f32),
            jax.ShapeDtypeStruct(chain_state.shape, f32),
        ],
        in_specs=[vmem, smem, vmem, vmem, vmem, hbm],
        out_specs=[hbm, hbm],
        scratch_shapes=[
            rows32,
            pltpu.VMEM(chain_state.shape, f32),
            pltpu.VMEM(chain_state.shape, f32),
            pltpu.VMEM(chain_state.shape, f32),
            dma((chains_loc,)),
            dma((chains_loc,)),
            dma((chains_loc,)),
        ],
        compiler_params=pltpu.CompilerParams(vmem_limit_bytes=18 * 2**20),
    )(table, temper, adj_all, state, moment, noise)


def on_device(chain_state, second_moment, noise, green, observed, inv_noise, temper):
    if fits_kernel(chain_state.shape, green.shape):
        return kernel_steps(
            chain_state, second_moment, noise, green, observed, inv_noise, temper
        )
    chains_loc, slab_rows, time_len = chain_state.shape
    freq_loc = green.shape[1]
    freq_count = lax.axis_size("freq")
    freq_total = freq_loc * freq_count
    chains = chains_loc * freq_count
    forward_table = spectral_table(time_len, freq_total)
    inverse_table = forward_table.T
    green_re = green[0]
    green_im = green[1]
    upper_rows = jnp.concatenate([green_re, green_im], axis=2)
    lower_rows = jnp.concatenate([-green_im, green_re], axis=2)
    kernel = jnp.concatenate([upper_rows, lower_rows], axis=1)
    weights = jnp.concatenate([inv_noise, inv_noise], axis=1)
    temper_cols = temper[:, None, None]
    current = chain_state
    moment = second_moment
    for step_num in range(noise.shape[0]):
        low_state = current.astype(jnp.bfloat16)
        local_spec = jnp.dot(
            low_state.reshape(chains_loc * slab_rows, time_len),
            forward_table,
            preferred_element_type=jnp.float32,
        )
        local_spec = local_spec.astype(jnp.bfloat16).reshape(chains_loc, slab_rows, 2 * freq_total)
        spectrum = lax.all_to_all(local_spec, "freq", split_axis=2, concat_axis=0, tiled=True)
        mixed_spec = (
            spectrum.reshape(chains, slab_rows, freq_loc, 2)
            .transpose(2, 0, 3, 1)
            .reshape(freq_loc, chains, 2 * slab_rows)
        )
        partial_data = jnp.einsum(
            "fcq,fqs->fcs", mixed_spec, kernel, preferred_element_type=jnp.float32
        )
        predicted = lax.psum(partial_data.astype(jnp.bfloat16), "param").astype(jnp.float32)
        weighted = (weights[:, None, :] * (predicted - observed[:, None, :])).astype(jnp.bfloat16)
        adjoint = jnp.einsum(
            "fcs,fqs->fcq", weighted, kernel, preferred_element_type=jnp.float32
        ).astype(jnp.bfloat16)
        adjoint = (
            adjoint.reshape(freq_loc, chains, 2, slab_rows)
            .transpose(1, 3, 0, 2)
            .reshape(chains, slab_rows, 2 * freq_loc)
        )
        own_adjoint = lax.all_to_all(adjoint, "freq", split_axis=0, concat_axis=2, tiled=True)
        gradient = jnp.dot(
            own_adjoint.reshape(chains_loc * slab_rows, 2 * freq_total),
            inverse_table,
            preferred_element_type=jnp.float32,
        )
        gradient = gradient.reshape(chains_loc, slab_rows, time_len)
        drift_term = temper_cols * gradient + current
        moment = decay_rate * moment + (1.0 - decay_rate) * drift_term * drift_term
        precondition = lax.rsqrt(moment)
        current = (
            current
            - step_length * precondition * drift_term
            + math.sqrt(2.0 * step_length) * jnp.sqrt(precondition) * noise[step_num]
        )
    return (current, moment)


def solution(mesh):
    return jax.shard_map(
        on_device,
        mesh=mesh,
        in_specs=(
            P("freq", "param", None),
            P("freq", "param", None),
            P(None, "freq", "param", None),
            P(None, "freq", "param", None),
            P("freq", None),
            P("freq", None),
            P("freq"),
        ),
        out_specs=(P("freq", "param", None), P("freq", "param", None)),
        check_vma=False,
    )
```

```python
import functools
import math

import jax
import jax.numpy as jnp
from jax import lax
from jax.experimental import pallas as pl
from jax.experimental.pallas import tpu as pltpu
from jax.sharding import PartitionSpec as P

decay_rate = 0.9
step_length = 0.5
MESH = pl.DeviceIdType.MESH
LANES = 128
GROUPS = 2
CHUNK_FREQS = 2
CORE_LAG = 2
HOP_LAG = 5
GATHER_LAG = 3
ADJ_LAG = 8
SPEC_LAG = 9


def spectral_table(time_len, freq_total):
    time_index = jnp.arange(time_len, dtype=jnp.int32)[:, None]
    wave_number = jnp.arange(freq_total, dtype=jnp.int32)[None, :] + 1
    phase_angle = (time_index * wave_number % time_len).astype(jnp.float32) * (
        2.0 * math.pi / time_len
    )
    columns_table = jnp.stack([jnp.cos(phase_angle), -jnp.sin(phase_angle)], axis=-1).reshape(
        time_len, 2 * freq_total
    )
    return (columns_table / math.sqrt(time_len)).astype(jnp.bfloat16)


def steps_kernel(
    freq_count, param_count, chunk_freqs,
    table_ref, temper_hbm, obs_hbm, inv_hbm, state_hbm, moment_hbm, noise_hbm, green_hbm,
    adj_all, state, moment,
    temper_ref, obs_all, inv_all, obs_rows, inv_rows, green, noise, rows32, spec, field, acc,
    core_out, core_in, up_out, up_in, down_out, down_in, wtd, adj,
    small_sem, state_sem, green_sem, moment_sem, noise_sem, spec_send, spec_recv,
    line_send, line_recv, adj_send, adj_recv,
):
    freq_me = lax.axis_index("freq")
    param_me = lax.axis_index("param")
    steps = noise.shape[0]
    groups = acc.shape[0]
    freq_loc = field.shape[1]
    rows, slab = field.shape[3], field.shape[4]
    group_chains = rows // 2
    all_rows, half = acc.shape[2], acc.shape[3]
    sensors = 2 * half
    col_blocks = slab // LANES
    columns = table_ref.shape[0]
    chunks = freq_loc // chunk_freqs
    line = param_count // 2
    core = lax.rem(param_me, 2)
    chip = param_me // 2
    core_peer = param_me + 1 - 2 * core
    above, below = param_me + 2, param_me - 2
    has_above, has_below = chip < line - 1, chip > 0
    peers = pl.ds(0, freq_count - 1)

    def freq_peer(d):
        return lax.rem(freq_me + d, freq_count)

    barrier = pltpu.get_barrier_semaphore()
    for d in range(1, freq_count):
        pl.semaphore_signal(barrier, inc=1, device_id={"freq": freq_peer(d)}, device_id_type=MESH)
    pl.semaphore_signal(barrier, inc=1, device_id={"param": core_peer}, device_id_type=MESH)

    @pl.when(has_above)
    def _():
        pl.semaphore_signal(barrier, inc=1, device_id={"param": above}, device_id_type=MESH)

    @pl.when(has_below)
    def _():
        pl.semaphore_signal(barrier, inc=1, device_id={"param": below}, device_id_type=MESH)

    def state_copy(c):
        return pltpu.make_async_copy(state_hbm.at[c], state.at[c], state_sem.at[c])

    def green_copy(f):
        return pltpu.make_async_copy(green_hbm.at[:, f], green.at[f], green_sem.at[f])

    def moment_copy(c):
        return pltpu.make_async_copy(moment_hbm.at[c], moment.at[c], moment_sem.at[0])

    def noise_copy(s, c):
        return pltpu.make_async_copy(noise_hbm.at[s, c], noise.at[s, c], noise_sem.at[s])

    def small_copy(k, src, dst):
        return pltpu.make_async_copy(src, dst, small_sem.at[k])

    def arrived(ref, sem):
        pltpu.make_async_copy(ref, ref, sem).wait()

    def freqs_of(i):
        return pl.ds(i * chunk_freqs, chunk_freqs)

    def spec_copy(q, g, i, d):
        return pltpu.make_async_remote_copy(
            src_ref=spec.at[q, freq_peer(d), freqs_of(i)],
            dst_ref=field.at[q, freqs_of(i), freq_me],
            send_sem=spec_send.at[0],
            recv_sem=spec_recv.at[g, i],
            device_id={"freq": freq_peer(d)},
            device_id_type=MESH,
        )

    def adj_copy(q, g, i, d):
        return pltpu.make_async_remote_copy(
            src_ref=adj.at[q, freqs_of(i), freq_peer(d)],
            dst_ref=adj_all.at[q, freq_me, freqs_of(i)],
            send_sem=adj_send.at[0],
            recv_sem=adj_recv.at[g],
            device_id={"freq": freq_peer(d)},
            device_id_type=MESH,
        )

    def param_copy(k, g, i, src, dst, peer):
        return pltpu.make_async_remote_copy(
            src_ref=src.at[freqs_of(i)],
            dst_ref=dst.at[freqs_of(i)],
            send_sem=line_send.at[k],
            recv_sem=line_recv.at[k, g, i],
            device_id={"param": peer},
            device_id_type=MESH,
        )

    def core_reduce(q, g, i):
        return param_copy(0, g, i, core_out.at[q], core_in.at[q], core_peer)

    def core_gather(q, g, i):
        return param_copy(1, g, i, wtd.at[q, core], wtd.at[q, core], core_peer)

    def up_copy(q, g, i):
        return param_copy(2, g, i, up_out.at[q], up_in.at[q], above)

    def down_copy(q, g, i):
        return param_copy(3, g, i, down_out.at[q], down_in.at[q], below)

    def transform(g, k, low):
        dims = (((1,), (1,)), ((), ()))
        result = lax.dot_general(table_ref[...], low, dims, preferred_element_type=jnp.float32)
        for b in range(col_blocks):
            block = result[:, b * LANES : (b + 1) * LANES]
            rows32[g, b, pl.ds(k, columns, stride=group_chains)] = block

    def send_spectrum(q, g):
        @pl.loop(0, chunks)
        def _(i):
            for d in range(freq_count):
                for e in range(chunk_freqs):
                    f = i * chunk_freqs + e
                    first = pl.multiple_of((freq_peer(d) * freq_loc + f) * rows, rows)
                    pieces = [rows32[g, b, pl.ds(first, rows)] for b in range(col_blocks)]
                    tile = jnp.concatenate(pieces, axis=1).astype(jnp.bfloat16)
                    if d == 0:
                        field[q, f, freq_me] = tile
                    else:
                        spec[q, freq_peer(d), f] = tile
            for d in range(1, freq_count):
                spec_copy(q, g, i, d).start()

    @pl.loop(0, groups * group_chains)
    def _(c):
        state_copy(c).start()

    smalls = ((temper_hbm, temper_ref), (obs_hbm, obs_all), (inv_hbm, inv_all))
    for k, (src, dst) in enumerate(smalls):
        small_copy(k, src, dst).start()

    met = has_above.astype(jnp.int32) + has_below.astype(jnp.int32)
    for g in range(groups):
        @pl.loop(0, group_chains)
        def _(k):
            c = g * group_chains + k
            state_copy(c).wait()
            transform(g, k, state[c].astype(jnp.bfloat16))

        if g == groups - 1:
            @pl.loop(0, freq_loc)
            def _(f):
                green_copy(f).start()

            @pl.loop(0, groups * group_chains)
            def _(c):
                moment_copy(c).start()
                for s in range(steps):
                    noise_copy(s, c).start()

        if g == 0:
            pl.semaphore_wait(barrier, freq_count + met)
        send_spectrum(g, g)

    for k, (src, dst) in enumerate(smalls):
        small_copy(k, src, dst).wait()
    for f in range(freq_loc):
        first = pl.multiple_of(core * half, half)
        inv_rows[f] = inv_all[f : f + 1, pl.ds(first, half)]
        for ri in range(2):
            first = pl.multiple_of(ri * sensors + core * half, half)
            target = obs_all[f : f + 1, pl.ds(first, half)]
            obs_rows[f, ri * group_chains : (ri + 1) * group_chains] = jnp.broadcast_to(
                target, (group_chains, half)
            )

    def turned(x, sign):
        wide = x.astype(jnp.float32).reshape(freq_count, rows, x.shape[-1])
        row = lax.broadcasted_iota(jnp.int32, wide.shape, 1)
        back = pltpu.roll(wide, group_chains, 1)
        flip = row < group_chains if sign > 0 else row >= group_chains
        return jnp.where(flip, -back, back).reshape(all_rows, x.shape[-1]).astype(jnp.bfloat16)

    def forward(s, n):
        g, i = lax.div(n, chunks), lax.rem(n, chunks)
        q = s * groups + g

        @pl.when((s == 0) & (g == 0))
        def _():
            for e in range(chunk_freqs):
                green_copy(i * chunk_freqs + e).wait()

        arrived(field.at[q, freqs_of(i), peers], spec_recv.at[g, i])
        for e in range(chunk_freqs):
            f = i * chunk_freqs + e
            wide = field[q, f].astype(jnp.float32).reshape(all_rows, slab)
            both = jnp.concatenate([wide.astype(jnp.bfloat16), turned(wide, 1)], axis=1)
            weights = green[f].reshape(2 * slab, sensors)
            data = jnp.dot(both, weights, preferred_element_type=jnp.float32)
            low, high = data[:, :half], data[:, half:]
            acc[g, f] = jnp.where(core == 0, low, high)
            core_out[q, f] = jnp.where(core == 0, high, low).astype(jnp.bfloat16)
        core_reduce(q, g, i).start()

    def merge(s, n):
        g, i = lax.div(n, chunks), lax.rem(n, chunks)
        q = s * groups + g
        core_reduce(q, g, i).wait_recv()
        total = acc[g, freqs_of(i)] + core_in[q, freqs_of(i)].astype(jnp.float32)
        acc[g, freqs_of(i)] = total

        @pl.when(chip == 0)
        def _():
            up_out[q, freqs_of(i)] = total.astype(jnp.bfloat16)
            up_copy(q, g, i).start()

        @pl.when(chip == line - 1)
        def _():
            down_out[q, freqs_of(i)] = total.astype(jnp.bfloat16)
            down_copy(q, g, i).start()

    def pass_up(s, n):
        g, i = lax.div(n, chunks), lax.rem(n, chunks)
        q = s * groups + g
        up_copy(q, g, i).wait_recv()
        total = acc[g, freqs_of(i)] + up_in[q, freqs_of(i)].astype(jnp.float32)
        up_out[q, freqs_of(i)] = total.astype(jnp.bfloat16)
        up_copy(q, g, i).start()

    def pass_down(s, n):
        g, i = lax.div(n, chunks), lax.rem(n, chunks)
        q = s * groups + g
        down_copy(q, g, i).wait_recv()
        total = acc[g, freqs_of(i)] + down_in[q, freqs_of(i)].astype(jnp.float32)
        down_out[q, freqs_of(i)] = total.astype(jnp.bfloat16)
        down_copy(q, g, i).start()

    def weigh(s, n):
        g, i = lax.div(n, chunks), lax.rem(n, chunks)
        q = s * groups + g

        @pl.when(chip == line - 1)
        def _():
            up_copy(q, g, i).wait_recv()

        @pl.when(chip == 0)
        def _():
            down_copy(q, g, i).wait_recv()

        @pl.when(has_below)
        def _():
            acc[g, freqs_of(i)] += up_in[q, freqs_of(i)].astype(jnp.float32)

        @pl.when(has_above)
        def _():
            acc[g, freqs_of(i)] += down_in[q, freqs_of(i)].astype(jnp.float32)

        for e in range(chunk_freqs):
            f = i * chunk_freqs + e
            apart = acc[g, f].reshape(freq_count, rows, half) - obs_rows[f][None]
            scaled = inv_rows[f][None] * apart
            wtd[q, core, f] = scaled.reshape(all_rows, half).astype(jnp.bfloat16)
        core_gather(q, g, i).start()

    def backward(s, n):
        g, i = lax.div(n, chunks), lax.rem(n, chunks)
        q = s * groups + g
        core_gather(q, g, i).wait_recv()
        dims = (((1,), (1,)), ((), ()))
        for e in range(chunk_freqs):
            f = i * chunk_freqs + e
            w = jnp.concatenate([wtd[q, 0, f], wtd[q, 1, f]], axis=1)
            first = lax.dot_general(w, green[f, 0], dims, preferred_element_type=jnp.float32)
            second = lax.dot_general(
                turned(w, -1), green[f, 1], dims, preferred_element_type=jnp.float32
            )
            back = (first + second).reshape(freq_count, rows, slab)
            adj[q, f] = back.astype(jnp.bfloat16)
            adj_all[q, freq_me, f] = adj[q, f, freq_me]
        for d in range(1, freq_count):
            adj_copy(q, g, i, d).start()

    def update(s, n):
        g, k = lax.div(n, chunks), lax.rem(n, chunks)
        q = s * groups + g
        going_on = s < steps - 1

        @pl.when((k < group_chains) & (going_on | (g < groups - 1)))
        def _():
            @pl.when(k == 0)
            def _():
                arrived(adj_all.at[q, peers], adj_recv.at[g])
                widen(adj_all.at[q], rows32.at[g])

                @pl.when(g == 0)
                def _():
                    @pl.when(s == 0)
                    def _():
                        arrived(moment, moment_sem.at[0])

                    arrived(noise.at[s], noise_sem.at[s])

            c = g * group_chains + k
            low = advance(
                k, c, rows32.at[g], table_ref, temper_ref, state, moment, noise.at[s], state, moment
            )

            @pl.when(going_on)
            def _():
                transform(g, k, low)

            @pl.when(going_on & (k == group_chains - 1))
            def _():
                send_spectrum(q + groups, g)

    span = groups * chunks
    up_lag = CORE_LAG + HOP_LAG * chip
    down_lag = CORE_LAG + HOP_LAG * (line - 1 - chip)
    weigh_lag = jnp.maximum(up_lag, down_lag)
    back_lag = CORE_LAG + HOP_LAG * (line - 1) + GATHER_LAG
    update_lag = back_lag + chunks - 1 + ADJ_LAG
    period = max(update_lag + group_chains - 1 + SPEC_LAG, span)
    inside = has_above & has_below
    total_ticks = (steps - 1) * period + max(
        span + back_lag, update_lag + (groups - 2) * chunks + group_chains
    )

    @pl.loop(0, total_ticks)
    def _(tick):
        def stage(lag, work, allowed=None):
            since = jnp.maximum(tick - lag, 0)
            s = lax.div(since, period)
            n = since - s * period
            due = (tick >= lag) & (s < steps) & (n < span)

            @pl.when(due if allowed is None else due & allowed)
            def _():
                work(s, n)

        stage(0, forward)
        stage(weigh_lag + GATHER_LAG, backward)
        stage(CORE_LAG, merge)
        stage(up_lag, pass_up, inside)
        stage(down_lag, pass_down, inside)
        stage(weigh_lag, weigh)
        stage(update_lag, update)

    last = steps * groups - 1
    arrived(adj_all.at[last, peers], adj_recv.at[groups - 1])
    arrived(spec.at[:, peers], spec_send.at[0])
    arrived(adj.at[:, :, peers], adj_send.at[0])
    for k in range(2):
        arrived(core_out, line_send.at[k])

    @pl.when(has_above)
    def _():
        arrived(core_out, line_send.at[2])

    @pl.when(has_below)
    def _():
        arrived(core_out, line_send.at[3])


def widen(adj, rows32):
    freq_count, freq_loc, rows, slab = adj.shape

    @pl.loop(0, freq_count)
    def _(j):
        for f in range(freq_loc):
            first = pl.multiple_of((j * freq_loc + f) * rows, rows)
            tile = adj[j, f].astype(jnp.float32)
            for b in range(slab // LANES):
                rows32[b, pl.ds(first, rows)] = tile[:, b * LANES : (b + 1) * LANES]


def advance(k, c, rows32, table_ref, temper_ref, state, moment, push, new_state, new_moment):
    columns, group_chains = table_ref.shape[0], rows32.shape[1] // table_ref.shape[0]
    pieces = [
        rows32[b, pl.ds(k, columns, stride=group_chains)] for b in range(rows32.shape[0])
    ]
    mine = jnp.concatenate(pieces, axis=1).T.astype(jnp.bfloat16)
    gradient = jnp.dot(mine, table_ref[...], preferred_element_type=jnp.float32)
    current = state[c]
    drift_term = temper_ref[c] * gradient + current
    spread = moment[c]
    spread = decay_rate * spread + (1.0 - decay_rate) * drift_term * drift_term
    precondition = lax.rsqrt(spread)
    root = precondition * lax.rsqrt(precondition)
    current = (
        current
        - step_length * precondition * drift_term
        + math.sqrt(2.0 * step_length) * root * push[c]
    )
    new_state[c] = current
    new_moment[c] = spread
    return current.astype(jnp.bfloat16)


def final_kernel(
    table_ref, temper_ref, adj_all, state, moment, noise_hbm, state_hbm, moment_hbm,
    rows32, push, new_state, new_moment, push_sem, state_sem, moment_sem,
):
    last, step = adj_all.shape[0] - 1, noise_hbm.shape[0] - 1
    left = new_state.shape[0]
    done = state.shape[0] - left

    def push_copy(k):
        return pltpu.make_async_copy(noise_hbm.at[step, done + k], push.at[k], push_sem.at[k])

    def state_copy(k):
        c = done + k
        return pltpu.make_async_copy(new_state.at[k], state_hbm.at[c], state_sem.at[c])

    def moment_copy(k):
        c = done + k
        return pltpu.make_async_copy(new_moment.at[k], moment_hbm.at[c], moment_sem.at[c])

    def done_state_copy(c):
        return pltpu.make_async_copy(state.at[c], state_hbm.at[c], state_sem.at[c])

    def done_moment_copy(c):
        return pltpu.make_async_copy(moment.at[c], moment_hbm.at[c], moment_sem.at[c])

    @pl.loop(0, left)
    def _(k):
        push_copy(k).start()

    @pl.loop(0, done)
    def _(c):
        done_state_copy(c).start()
        done_moment_copy(c).start()

    widen(adj_all.at[last], rows32)

    @pl.loop(0, left)
    def _(k):
        push_copy(k).wait()
        advance(
            k, k, rows32, table_ref, temper_ref.at[pl.ds(done, left)], state.at[pl.ds(done, left)],
            moment.at[pl.ds(done, left)], push, new_state, new_moment,
        )
        state_copy(k).start()
        moment_copy(k).start()

    @pl.loop(0, done)
    def _(c):
        done_state_copy(c).wait()
        done_moment_copy(c).wait()

    @pl.loop(0, left)
    def _(k):
        state_copy(k).wait()
        moment_copy(k).wait()


def fits_kernel(chain_shape, green_shape):
    chains_loc, slab = chain_shape[0], chain_shape[1]
    param_count = lax.axis_size("param")
    return (
        chains_loc % GROUPS == 0
        and 2 * (chains_loc // GROUPS) % 8 == 0
        and slab % LANES == 0
        and chain_shape[2] % LANES == 0
        and green_shape[3] % (2 * LANES) == 0
        and green_shape[1] % CHUNK_FREQS == 0
        and green_shape[1] // CHUNK_FREQS >= chains_loc // GROUPS
        and param_count == 8
        and lax.axis_size("freq") > 1
    )


def kernel_steps(chain_state, second_moment, noise, green, observed, inv_noise, temper):
    chains_loc, slab, time_len = chain_state.shape
    freq_loc, sensors = green.shape[1], green.shape[3]
    steps = noise.shape[0]
    freq_count, param_count = lax.axis_size("freq"), lax.axis_size("param")
    columns = 2 * freq_loc * freq_count
    table = spectral_table(time_len, freq_loc * freq_count).T
    chunks = freq_loc // CHUNK_FREQS
    group_chains = chains_loc // GROUPS
    rows, half = 2 * group_chains, sensors // 2
    all_rows = freq_count * rows
    items = steps * GROUPS
    bf16, f32 = jnp.bfloat16, jnp.float32
    dma = pltpu.SemaphoreType.DMA
    vmem = pl.BlockSpec(memory_space=pltpu.VMEM)
    smem = pl.BlockSpec(memory_space=pltpu.SMEM)
    hbm = pl.BlockSpec(memory_space=pltpu.HBM)
    line_buf = pltpu.VMEM((items, freq_loc, all_rows, half), bf16)
    rows32 = (slab // LANES, columns * group_chains, LANES)
    part = (group_chains, slab, time_len)
    observed, inv_noise, temper_hbm, noise = (
        pltpu.with_memory_space_constraint(x, pltpu.HBM)
        for x in (observed, inv_noise, temper, noise)
    )
    adj_all, state, moment = pl.pallas_call(
        functools.partial(steps_kernel, freq_count, param_count, CHUNK_FREQS),
        out_shape=[
            jax.ShapeDtypeStruct((items, freq_count, freq_loc, rows, slab), bf16),
            jax.ShapeDtypeStruct(chain_state.shape, f32),
            jax.ShapeDtypeStruct(chain_state.shape, f32),
        ],
        in_specs=[vmem, hbm, hbm, hbm, hbm, hbm, hbm, hbm],
        out_specs=[vmem, vmem, vmem],
        scratch_shapes=[
            pltpu.SMEM(temper.shape, f32),
            pltpu.VMEM(observed.shape, f32),
            pltpu.VMEM(inv_noise.shape, f32),
            pltpu.VMEM((freq_loc, rows, half), f32),
            pltpu.VMEM((freq_loc, 1, half), f32),
            pltpu.VMEM((freq_loc, 2, slab, sensors), bf16),
            pltpu.VMEM((steps,) + chain_state.shape, f32),
            pltpu.VMEM((GROUPS,) + rows32, f32),
            pltpu.VMEM((items, freq_count, freq_loc, rows, slab), bf16),
            pltpu.VMEM((items, freq_loc, freq_count, rows, slab), bf16),
            pltpu.VMEM((GROUPS, freq_loc, all_rows, half), f32),
            line_buf, line_buf, line_buf, line_buf, line_buf, line_buf,
            pltpu.VMEM((items, 2, freq_loc, all_rows, half), bf16),
            pltpu.VMEM((items, freq_loc, freq_count, rows, slab), bf16),
            dma((3,)),
            dma((chains_loc,)),
            dma((freq_loc,)),
            dma((1,)),
            dma((steps,)),
            dma((1,)),
            dma((GROUPS, chunks)),
            dma((4,)),
            dma((4, GROUPS, chunks)),
            dma((1,)),
            dma((GROUPS,)),
        ],
        compiler_params=pltpu.CompilerParams(
            collective_id=0, has_side_effects=True, vmem_limit_bytes=44 * 2**20
        ),
    )(table, temper_hbm, observed, inv_noise, chain_state, second_moment, noise, green)
    return pl.pallas_call(
        final_kernel,
        out_shape=[
            jax.ShapeDtypeStruct(chain_state.shape, f32),
            jax.ShapeDtypeStruct(chain_state.shape, f32),
        ],
        in_specs=[vmem, smem, vmem, vmem, vmem, hbm],
        out_specs=[hbm, hbm],
        scratch_shapes=[
            pltpu.VMEM(rows32, f32),
            pltpu.VMEM(part, f32),
            pltpu.VMEM(part, f32),
            pltpu.VMEM(part, f32),
            dma((group_chains,)),
            dma((chains_loc,)),
            dma((chains_loc,)),
        ],
        compiler_params=pltpu.CompilerParams(vmem_limit_bytes=18 * 2**20),
    )(table, temper, adj_all, state, moment, noise)


def on_device(chain_state, second_moment, noise, green, observed, inv_noise, temper):
    if fits_kernel(chain_state.shape, green.shape):
        return kernel_steps(
            chain_state, second_moment, noise, green, observed, inv_noise, temper
        )
    chains_loc, slab_rows, time_len = chain_state.shape
    freq_loc = green.shape[1]
    freq_count = lax.axis_size("freq")
    freq_total = freq_loc * freq_count
    chains = chains_loc * freq_count
    forward_table = spectral_table(time_len, freq_total)
    inverse_table = forward_table.T
    green_re = green[0]
    green_im = green[1]
    upper_rows = jnp.concatenate([green_re, green_im], axis=2)
    lower_rows = jnp.concatenate([-green_im, green_re], axis=2)
    kernel = jnp.concatenate([upper_rows, lower_rows], axis=1)
    weights = jnp.concatenate([inv_noise, inv_noise], axis=1)
    temper_cols = temper[:, None, None]
    current = chain_state
    moment = second_moment
    for step_num in range(noise.shape[0]):
        low_state = current.astype(jnp.bfloat16)
        local_spec = jnp.dot(
            low_state.reshape(chains_loc * slab_rows, time_len),
            forward_table,
            preferred_element_type=jnp.float32,
        )
        local_spec = local_spec.astype(jnp.bfloat16).reshape(chains_loc, slab_rows, 2 * freq_total)
        spectrum = lax.all_to_all(local_spec, "freq", split_axis=2, concat_axis=0, tiled=True)
        mixed_spec = (
            spectrum.reshape(chains, slab_rows, freq_loc, 2)
            .transpose(2, 0, 3, 1)
            .reshape(freq_loc, chains, 2 * slab_rows)
        )
        partial_data = jnp.einsum(
            "fcq,fqs->fcs", mixed_spec, kernel, preferred_element_type=jnp.float32
        )
        predicted = lax.psum(partial_data.astype(jnp.bfloat16), "param").astype(jnp.float32)
        weighted = (weights[:, None, :] * (predicted - observed[:, None, :])).astype(jnp.bfloat16)
        adjoint = jnp.einsum(
            "fcs,fqs->fcq", weighted, kernel, preferred_element_type=jnp.float32
        ).astype(jnp.bfloat16)
        adjoint = (
            adjoint.reshape(freq_loc, chains, 2, slab_rows)
            .transpose(1, 3, 0, 2)
            .reshape(chains, slab_rows, 2 * freq_loc)
        )
        own_adjoint = lax.all_to_all(adjoint, "freq", split_axis=0, concat_axis=2, tiled=True)
        gradient = jnp.dot(
            own_adjoint.reshape(chains_loc * slab_rows, 2 * freq_total),
            inverse_table,
            preferred_element_type=jnp.float32,
        )
        gradient = gradient.reshape(chains_loc, slab_rows, time_len)
        drift_term = temper_cols * gradient + current
        moment = decay_rate * moment + (1.0 - decay_rate) * drift_term * drift_term
        precondition = lax.rsqrt(moment)
        current = (
            current
            - step_length * precondition * drift_term
            + math.sqrt(2.0 * step_length) * jnp.sqrt(precondition) * noise[step_num]
        )
    return (current, moment)


def solution(mesh):
    return jax.shard_map(
        on_device,
        mesh=mesh,
        in_specs=(
            P("freq", "param", None),
            P("freq", "param", None),
            P(None, "freq", "param", None),
            P(None, "freq", "param", None),
            P("freq", None),
            P("freq", None),
            P("freq"),
        ),
        out_specs=(P("freq", "param", None), P("freq", "param", None)),
        check_vma=False,
    )
```

```python
import functools
import math

import jax
import jax.numpy as jnp
from jax import lax
from jax.experimental import pallas as pl
from jax.experimental.pallas import tpu as pltpu
from jax.sharding import PartitionSpec as P

decay_rate = 0.9
step_length = 0.5
MESH = pl.DeviceIdType.MESH
LANES = 128
GROUPS = 2
CHUNK_FREQS = 2
CORE_LAG = 2
HOP_LAG = 5
GATHER_LAG = 3
ADJ_LAG = 8
SPEC_LAG = 9
TABLE_ROWS = 16


def spectral_table(time_len, freq_total):
    time_index = jnp.arange(time_len, dtype=jnp.int32)[:, None]
    wave_number = jnp.arange(freq_total, dtype=jnp.int32)[None, :] + 1
    phase_angle = (time_index * wave_number % time_len).astype(jnp.float32) * (
        2.0 * math.pi / time_len
    )
    columns_table = jnp.stack([jnp.cos(phase_angle), -jnp.sin(phase_angle)], axis=-1).reshape(
        time_len, 2 * freq_total
    )
    return (columns_table / math.sqrt(time_len)).astype(jnp.bfloat16)


def steps_kernel(
    freq_count, param_count, chunk_freqs,
    temper_hbm, obs_hbm, inv_hbm, state_hbm, moment_hbm, noise_hbm, green_hbm,
    adj_all, state, moment, push, table_ref,
    temper_ref, obs_all, inv_all, obs_rows, inv_rows, green, noise, rows32, spec, field, acc,
    core_out, core_in, up_out, up_in, down_out, down_in, wtd, adj,
    small_sem, state_sem, green_sem, moment_sem, noise_sem, push_sem, spec_send, spec_recv,
    line_send, line_recv, adj_send, adj_recv,
):
    freq_me = lax.axis_index("freq")
    param_me = lax.axis_index("param")
    steps = noise.shape[0]
    groups = acc.shape[0]
    freq_loc = field.shape[1]
    rows, slab = field.shape[3], field.shape[4]
    group_chains = rows // 2
    all_rows, half = acc.shape[2], acc.shape[3]
    sensors = 2 * half
    col_blocks = slab // LANES
    columns = table_ref.shape[0]
    chunks = freq_loc // chunk_freqs
    line = param_count // 2
    core = lax.rem(param_me, 2)
    chip = param_me // 2
    core_peer = param_me + 1 - 2 * core
    above, below = param_me + 2, param_me - 2
    has_above, has_below = chip < line - 1, chip > 0
    peers = pl.ds(0, freq_count - 1)

    def freq_peer(d):
        return lax.rem(freq_me + d, freq_count)

    barrier = pltpu.get_barrier_semaphore()
    for d in range(1, freq_count):
        pl.semaphore_signal(barrier, inc=1, device_id={"freq": freq_peer(d)}, device_id_type=MESH)
    pl.semaphore_signal(barrier, inc=1, device_id={"param": core_peer}, device_id_type=MESH)

    @pl.when(has_above)
    def _():
        pl.semaphore_signal(barrier, inc=1, device_id={"param": above}, device_id_type=MESH)

    @pl.when(has_below)
    def _():
        pl.semaphore_signal(barrier, inc=1, device_id={"param": below}, device_id_type=MESH)

    def state_copy(c):
        return pltpu.make_async_copy(state_hbm.at[c], state.at[c], state_sem.at[c])

    def green_copy(f):
        return pltpu.make_async_copy(green_hbm.at[:, f], green.at[f], green_sem.at[f])

    def moment_copy(c):
        return pltpu.make_async_copy(moment_hbm.at[c], moment.at[c], moment_sem.at[0])

    def noise_copy(s, c):
        return pltpu.make_async_copy(noise_hbm.at[s, c], noise.at[s, c], noise_sem.at[s])

    def push_copy():
        left = pl.ds((groups - 1) * group_chains, group_chains)
        return pltpu.make_async_copy(noise_hbm.at[steps - 1, left], push, push_sem.at[0])

    def small_copy(k, src, dst):
        return pltpu.make_async_copy(src, dst, small_sem.at[k])

    def arrived(ref, sem):
        pltpu.make_async_copy(ref, ref, sem).wait()

    def freqs_of(i):
        return pl.ds(i * chunk_freqs, chunk_freqs)

    def spec_copy(q, g, i, d):
        return pltpu.make_async_remote_copy(
            src_ref=spec.at[q, freq_peer(d), freqs_of(i)],
            dst_ref=field.at[q, freqs_of(i), freq_me],
            send_sem=spec_send.at[0],
            recv_sem=spec_recv.at[g, i],
            device_id={"freq": freq_peer(d)},
            device_id_type=MESH,
        )

    def adj_copy(q, g, i, d):
        return pltpu.make_async_remote_copy(
            src_ref=adj.at[q, freqs_of(i), freq_peer(d)],
            dst_ref=adj_all.at[q, freq_me, freqs_of(i)],
            send_sem=adj_send.at[0],
            recv_sem=adj_recv.at[g],
            device_id={"freq": freq_peer(d)},
            device_id_type=MESH,
        )

    def param_copy(k, g, i, src, dst, peer):
        return pltpu.make_async_remote_copy(
            src_ref=src.at[freqs_of(i)],
            dst_ref=dst.at[freqs_of(i)],
            send_sem=line_send.at[k],
            recv_sem=line_recv.at[k, g, i],
            device_id={"param": peer},
            device_id_type=MESH,
        )

    def core_reduce(q, g, i):
        return param_copy(0, g, i, core_out.at[q], core_in.at[q], core_peer)

    def core_gather(q, g, i):
        return param_copy(1, g, i, wtd.at[q, core], wtd.at[q, core], core_peer)

    def up_copy(q, g, i):
        return param_copy(2, g, i, up_out.at[q], up_in.at[q], above)

    def down_copy(q, g, i):
        return param_copy(3, g, i, down_out.at[q], down_in.at[q], below)

    def transform(g, k, low):
        dims = (((1,), (1,)), ((), ()))
        result = lax.dot_general(table_ref[...], low, dims, preferred_element_type=jnp.float32)
        for b in range(col_blocks):
            block = result[:, b * LANES : (b + 1) * LANES]
            rows32[g, b, pl.ds(k, columns, stride=group_chains)] = block

    def send_spectrum(q, g):
        @pl.loop(0, chunks)
        def _(i):
            for d in range(freq_count):
                for e in range(chunk_freqs):
                    f = i * chunk_freqs + e
                    first = pl.multiple_of((freq_peer(d) * freq_loc + f) * rows, rows)
                    pieces = [rows32[g, b, pl.ds(first, rows)] for b in range(col_blocks)]
                    tile = jnp.concatenate(pieces, axis=1).astype(jnp.bfloat16)
                    if d == 0:
                        field[q, f, freq_me] = tile
                    else:
                        spec[q, freq_peer(d), f] = tile
            for d in range(1, freq_count):
                spec_copy(q, g, i, d).start()

    @pl.loop(0, group_chains)
    def _(c):
        state_copy(c).start()

    smalls = ((temper_hbm, temper_ref), (obs_hbm, obs_all), (inv_hbm, inv_all))
    for k, (src, dst) in enumerate(smalls):
        small_copy(k, src, dst).start()

    fill_table(table_ref)
    met = has_above.astype(jnp.int32) + has_below.astype(jnp.int32)
    for g in range(groups):
        @pl.loop(0, group_chains)
        def _(k):
            c = g * group_chains + k
            state_copy(c).wait()
            if g < groups - 1:
                state_copy(c + group_chains).start()
            transform(g, k, state[c].astype(jnp.bfloat16))

        if g == groups - 1:
            @pl.loop(0, freq_loc)
            def _(f):
                green_copy(f).start()

            @pl.loop(0, groups * group_chains)
            def _(c):
                moment_copy(c).start()
                for s in range(steps - 1):
                    noise_copy(s, c).start()

            @pl.loop(0, (groups - 1) * group_chains)
            def _(c):
                noise_copy(steps - 1, c).start()

            push_copy().start()

        if g == 0:
            pl.semaphore_wait(barrier, freq_count + met)
        send_spectrum(g, g)

    for k, (src, dst) in enumerate(smalls):
        small_copy(k, src, dst).wait()
    for f in range(freq_loc):
        first = pl.multiple_of(core * half, half)
        inv_rows[f] = inv_all[f : f + 1, pl.ds(first, half)]
        for ri in range(2):
            first = pl.multiple_of(ri * sensors + core * half, half)
            target = obs_all[f : f + 1, pl.ds(first, half)]
            obs_rows[f, ri * group_chains : (ri + 1) * group_chains] = jnp.broadcast_to(
                target, (group_chains, half)
            )

    def turned(x, sign):
        wide = x.astype(jnp.float32).reshape(freq_count, rows, x.shape[-1])
        row = lax.broadcasted_iota(jnp.int32, wide.shape, 1)
        back = pltpu.roll(wide, group_chains, 1)
        flip = row < group_chains if sign > 0 else row >= group_chains
        return jnp.where(flip, -back, back).reshape(all_rows, x.shape[-1]).astype(jnp.bfloat16)

    def forward(s, n):
        g, i = lax.div(n, chunks), lax.rem(n, chunks)
        q = s * groups + g

        @pl.when((s == 0) & (g == 0))
        def _():
            for e in range(chunk_freqs):
                green_copy(i * chunk_freqs + e).wait()

        arrived(field.at[q, freqs_of(i), peers], spec_recv.at[g, i])
        for e in range(chunk_freqs):
            f = i * chunk_freqs + e
            wide = field[q, f].astype(jnp.float32).reshape(all_rows, slab)
            both = jnp.concatenate([wide.astype(jnp.bfloat16), turned(wide, 1)], axis=1)
            weights = green[f].reshape(2 * slab, sensors)
            data = jnp.dot(both, weights, preferred_element_type=jnp.float32)
            low, high = data[:, :half], data[:, half:]
            acc[g, f] = jnp.where(core == 0, low, high)
            core_out[q, f] = jnp.where(core == 0, high, low).astype(jnp.bfloat16)
        core_reduce(q, g, i).start()

    def merge(s, n):
        g, i = lax.div(n, chunks), lax.rem(n, chunks)
        q = s * groups + g
        core_reduce(q, g, i).wait_recv()
        total = acc[g, freqs_of(i)] + core_in[q, freqs_of(i)].astype(jnp.float32)
        acc[g, freqs_of(i)] = total

        @pl.when(chip == 0)
        def _():
            up_out[q, freqs_of(i)] = total.astype(jnp.bfloat16)
            up_copy(q, g, i).start()

        @pl.when(chip == line - 1)
        def _():
            down_out[q, freqs_of(i)] = total.astype(jnp.bfloat16)
            down_copy(q, g, i).start()

    def pass_up(s, n):
        g, i = lax.div(n, chunks), lax.rem(n, chunks)
        q = s * groups + g
        up_copy(q, g, i).wait_recv()
        total = acc[g, freqs_of(i)] + up_in[q, freqs_of(i)].astype(jnp.float32)
        up_out[q, freqs_of(i)] = total.astype(jnp.bfloat16)
        up_copy(q, g, i).start()

    def pass_down(s, n):
        g, i = lax.div(n, chunks), lax.rem(n, chunks)
        q = s * groups + g
        down_copy(q, g, i).wait_recv()
        total = acc[g, freqs_of(i)] + down_in[q, freqs_of(i)].astype(jnp.float32)
        down_out[q, freqs_of(i)] = total.astype(jnp.bfloat16)
        down_copy(q, g, i).start()

    def weigh(s, n):
        g, i = lax.div(n, chunks), lax.rem(n, chunks)
        q = s * groups + g

        @pl.when(chip == line - 1)
        def _():
            up_copy(q, g, i).wait_recv()

        @pl.when(chip == 0)
        def _():
            down_copy(q, g, i).wait_recv()

        @pl.when(has_below)
        def _():
            acc[g, freqs_of(i)] += up_in[q, freqs_of(i)].astype(jnp.float32)

        @pl.when(has_above)
        def _():
            acc[g, freqs_of(i)] += down_in[q, freqs_of(i)].astype(jnp.float32)

        for e in range(chunk_freqs):
            f = i * chunk_freqs + e
            apart = acc[g, f].reshape(freq_count, rows, half) - obs_rows[f][None]
            scaled = inv_rows[f][None] * apart
            wtd[q, core, f] = scaled.reshape(all_rows, half).astype(jnp.bfloat16)
        core_gather(q, g, i).start()

    def backward(s, n):
        g, i = lax.div(n, chunks), lax.rem(n, chunks)
        q = s * groups + g
        core_gather(q, g, i).wait_recv()
        dims = (((1,), (1,)), ((), ()))
        for e in range(chunk_freqs):
            f = i * chunk_freqs + e
            w = jnp.concatenate([wtd[q, 0, f], wtd[q, 1, f]], axis=1)
            first = lax.dot_general(w, green[f, 0], dims, preferred_element_type=jnp.float32)
            second = lax.dot_general(
                turned(w, -1), green[f, 1], dims, preferred_element_type=jnp.float32
            )
            back = (first + second).reshape(freq_count, rows, slab)
            adj[q, f] = back.astype(jnp.bfloat16)
            adj_all[q, freq_me, f] = adj[q, f, freq_me]
        for d in range(1, freq_count):
            adj_copy(q, g, i, d).start()

    def update(s, n):
        g, k = lax.div(n, chunks), lax.rem(n, chunks)
        q = s * groups + g
        going_on = s < steps - 1

        @pl.when((k < group_chains) & (going_on | (g < groups - 1)))
        def _():
            @pl.when(k == 0)
            def _():
                arrived(adj_all.at[q, peers], adj_recv.at[g])
                widen(adj_all.at[q], rows32.at[g])

                @pl.when(g == 0)
                def _():
                    @pl.when(s == 0)
                    def _():
                        arrived(moment, moment_sem.at[0])

                    @pl.when(going_on)
                    def _():
                        arrived(noise.at[s], noise_sem.at[s])

                    @pl.when(s == steps - 1)
                    def _():
                        read = pl.ds(0, (groups - 1) * group_chains)
                        arrived(noise.at[s, read], noise_sem.at[s])

            c = g * group_chains + k
            low = advance(
                k, c, rows32.at[g], table_ref, temper_ref, state, moment, noise.at[s], state, moment
            )

            @pl.when(going_on)
            def _():
                transform(g, k, low)

            @pl.when(going_on & (k == group_chains - 1))
            def _():
                send_spectrum(q + groups, g)

    span = groups * chunks
    up_lag = CORE_LAG + HOP_LAG * chip
    down_lag = CORE_LAG + HOP_LAG * (line - 1 - chip)
    weigh_lag = jnp.maximum(up_lag, down_lag)
    back_lag = CORE_LAG + HOP_LAG * (line - 1) + GATHER_LAG
    update_lag = back_lag + chunks - 1 + ADJ_LAG
    period = max(update_lag + group_chains - 1 + SPEC_LAG, span)
    inside = has_above & has_below
    total_ticks = (steps - 1) * period + max(
        span + back_lag, update_lag + (groups - 2) * chunks + group_chains
    )

    @pl.loop(0, total_ticks)
    def _(tick):
        def stage(lag, work, allowed=None):
            since = jnp.maximum(tick - lag, 0)
            s = lax.div(since, period)
            n = since - s * period
            due = (tick >= lag) & (s < steps) & (n < span)

            @pl.when(due if allowed is None else due & allowed)
            def _():
                work(s, n)

        stage(0, forward)
        stage(weigh_lag + GATHER_LAG, backward)
        stage(CORE_LAG, merge)
        stage(up_lag, pass_up, inside)
        stage(down_lag, pass_down, inside)
        stage(weigh_lag, weigh)
        stage(update_lag, update)

    last = steps * groups - 1
    push_copy().wait()
    arrived(adj_all.at[last, peers], adj_recv.at[groups - 1])
    arrived(spec.at[:, peers], spec_send.at[0])
    arrived(adj.at[:, :, peers], adj_send.at[0])
    for k in range(2):
        arrived(core_out, line_send.at[k])

    @pl.when(has_above)
    def _():
        arrived(core_out, line_send.at[2])

    @pl.when(has_below)
    def _():
        arrived(core_out, line_send.at[3])


def fill_table(table_ref):
    columns, time_len = table_ref.shape

    @pl.loop(0, columns // TABLE_ROWS)
    def _(i):
        first = pl.multiple_of(i * TABLE_ROWS, TABLE_ROWS)
        column = lax.broadcasted_iota(jnp.int32, (TABLE_ROWS, time_len), 0) + first
        time_index = lax.broadcasted_iota(jnp.int32, (TABLE_ROWS, time_len), 1)
        turn = time_index * ((column >> 1) + 1) + (column & 1) * (time_len // 4)
        phase_angle = (turn & (time_len - 1)).astype(jnp.float32) * (2.0 * math.pi / time_len)
        rows = jnp.cos(phase_angle) / math.sqrt(time_len)
        table_ref[pl.ds(first, TABLE_ROWS)] = rows.astype(jnp.bfloat16)


def widen(adj, rows32):
    freq_count, freq_loc, rows, slab = adj.shape

    @pl.loop(0, freq_count)
    def _(j):
        for f in range(freq_loc):
            first = pl.multiple_of((j * freq_loc + f) * rows, rows)
            tile = adj[j, f].astype(jnp.float32)
            for b in range(slab // LANES):
                rows32[b, pl.ds(first, rows)] = tile[:, b * LANES : (b + 1) * LANES]


def advance(k, c, rows32, table_ref, temper_ref, state, moment, push, new_state, new_moment):
    columns, group_chains = table_ref.shape[0], rows32.shape[1] // table_ref.shape[0]
    pieces = [
        rows32[b, pl.ds(k, columns, stride=group_chains)] for b in range(rows32.shape[0])
    ]
    mine = jnp.concatenate(pieces, axis=1).T.astype(jnp.bfloat16)
    gradient = jnp.dot(mine, table_ref[...], preferred_element_type=jnp.float32)
    current = state[c]
    drift_term = temper_ref[c] * gradient + current
    spread = moment[c]
    spread = decay_rate * spread + (1.0 - decay_rate) * drift_term * drift_term
    precondition = lax.rsqrt(spread)
    root = precondition * lax.rsqrt(precondition)
    current = (
        current
        - step_length * precondition * drift_term
        + math.sqrt(2.0 * step_length) * root * push[c]
    )
    new_state[c] = current
    new_moment[c] = spread
    return current.astype(jnp.bfloat16)


def final_kernel(
    table_ref, temper_ref, adj_all, state, moment, push, state_hbm, moment_hbm,
    rows32, new_state, new_moment, state_sem, moment_sem,
):
    last = adj_all.shape[0] - 1
    left = new_state.shape[0]
    done = state.shape[0] - left

    def state_copy(k):
        c = done + k
        return pltpu.make_async_copy(new_state.at[k], state_hbm.at[c], state_sem.at[c])

    def moment_copy(k):
        c = done + k
        return pltpu.make_async_copy(new_moment.at[k], moment_hbm.at[c], moment_sem.at[c])

    def done_state_copy(c):
        return pltpu.make_async_copy(state.at[c], state_hbm.at[c], state_sem.at[c])

    def done_moment_copy(c):
        return pltpu.make_async_copy(moment.at[c], moment_hbm.at[c], moment_sem.at[c])

    @pl.loop(0, done)
    def _(c):
        done_state_copy(c).start()
        done_moment_copy(c).start()

    widen(adj_all.at[last], rows32)

    @pl.loop(0, left)
    def _(k):
        here = pl.ds(done, left)
        advance(
            k, k, rows32, table_ref, temper_ref.at[here], state.at[here], moment.at[here],
            push, new_state, new_moment,
        )
        state_copy(k).start()
        moment_copy(k).start()

    @pl.loop(0, done)
    def _(c):
        done_state_copy(c).wait()
        done_moment_copy(c).wait()

    @pl.loop(0, left)
    def _(k):
        state_copy(k).wait()
        moment_copy(k).wait()


def fits_kernel(chain_shape, green_shape):
    chains_loc, slab = chain_shape[0], chain_shape[1]
    param_count = lax.axis_size("param")
    return (
        chains_loc % GROUPS == 0
        and 2 * (chains_loc // GROUPS) % 8 == 0
        and slab % LANES == 0
        and chain_shape[2] % LANES == 0
        and chain_shape[2] & (chain_shape[2] - 1) == 0
        and 2 * green_shape[1] * lax.axis_size("freq") % TABLE_ROWS == 0
        and green_shape[3] % (2 * LANES) == 0
        and green_shape[1] % CHUNK_FREQS == 0
        and green_shape[1] // CHUNK_FREQS >= chains_loc // GROUPS
        and param_count == 8
        and lax.axis_size("freq") > 1
    )


def kernel_steps(chain_state, second_moment, noise, green, observed, inv_noise, temper):
    chains_loc, slab, time_len = chain_state.shape
    freq_loc, sensors = green.shape[1], green.shape[3]
    steps = noise.shape[0]
    freq_count, param_count = lax.axis_size("freq"), lax.axis_size("param")
    columns = 2 * freq_loc * freq_count
    chunks = freq_loc // CHUNK_FREQS
    group_chains = chains_loc // GROUPS
    rows, half = 2 * group_chains, sensors // 2
    all_rows = freq_count * rows
    items = steps * GROUPS
    bf16, f32 = jnp.bfloat16, jnp.float32
    dma = pltpu.SemaphoreType.DMA
    vmem = pl.BlockSpec(memory_space=pltpu.VMEM)
    smem = pl.BlockSpec(memory_space=pltpu.SMEM)
    hbm = pl.BlockSpec(memory_space=pltpu.HBM)
    line_buf = pltpu.VMEM((items, freq_loc, all_rows, half), bf16)
    rows32 = (slab // LANES, columns * group_chains, LANES)
    part = (group_chains, slab, time_len)
    operands = [
        pltpu.with_memory_space_constraint(x, pltpu.HBM)
        for x in (temper, observed, inv_noise, chain_state, second_moment, noise, green)
    ]
    adj_all, state, moment, push, table = pl.pallas_call(
        functools.partial(steps_kernel, freq_count, param_count, CHUNK_FREQS),
        out_shape=[
            jax.ShapeDtypeStruct((items, freq_count, freq_loc, rows, slab), bf16),
            jax.ShapeDtypeStruct(chain_state.shape, f32),
            jax.ShapeDtypeStruct(chain_state.shape, f32),
            jax.ShapeDtypeStruct(part, f32),
            jax.ShapeDtypeStruct((columns, time_len), bf16),
        ],
        in_specs=[hbm, hbm, hbm, hbm, hbm, hbm, hbm],
        out_specs=[vmem, vmem, vmem, vmem, vmem],
        scratch_shapes=[
            pltpu.SMEM(temper.shape, f32),
            pltpu.VMEM(observed.shape, f32),
            pltpu.VMEM(inv_noise.shape, f32),
            pltpu.VMEM((freq_loc, rows, half), f32),
            pltpu.VMEM((freq_loc, 1, half), f32),
            pltpu.VMEM((freq_loc, 2, slab, sensors), bf16),
            pltpu.VMEM((steps,) + chain_state.shape, f32),
            pltpu.VMEM((GROUPS,) + rows32, f32),
            pltpu.VMEM((items, freq_count, freq_loc, rows, slab), bf16),
            pltpu.VMEM((items, freq_loc, freq_count, rows, slab), bf16),
            pltpu.VMEM((GROUPS, freq_loc, all_rows, half), f32),
            line_buf, line_buf, line_buf, line_buf, line_buf, line_buf,
            pltpu.VMEM((items, 2, freq_loc, all_rows, half), bf16),
            pltpu.VMEM((items, freq_loc, freq_count, rows, slab), bf16),
            dma((3,)),
            dma((chains_loc,)),
            dma((freq_loc,)),
            dma((1,)),
            dma((steps,)),
            dma((1,)),
            dma((1,)),
            dma((GROUPS, chunks)),
            dma((4,)),
            dma((4, GROUPS, chunks)),
            dma((1,)),
            dma((GROUPS,)),
        ],
        compiler_params=pltpu.CompilerParams(
            collective_id=0, has_side_effects=True, vmem_limit_bytes=36 * 2**20
        ),
    )(*operands)
    return pl.pallas_call(
        final_kernel,
        out_shape=[
            jax.ShapeDtypeStruct(chain_state.shape, f32),
            jax.ShapeDtypeStruct(chain_state.shape, f32),
        ],
        in_specs=[vmem, smem, vmem, vmem, vmem, vmem],
        out_specs=[hbm, hbm],
        scratch_shapes=[
            pltpu.VMEM(rows32, f32),
            pltpu.VMEM(part, f32),
            pltpu.VMEM(part, f32),
            dma((chains_loc,)),
            dma((chains_loc,)),
        ],
        compiler_params=pltpu.CompilerParams(vmem_limit_bytes=8 * 2**20),
    )(table, temper, adj_all, state, moment, push)


def on_device(chain_state, second_moment, noise, green, observed, inv_noise, temper):
    if fits_kernel(chain_state.shape, green.shape):
        return kernel_steps(
            chain_state, second_moment, noise, green, observed, inv_noise, temper
        )
    chains_loc, slab_rows, time_len = chain_state.shape
    freq_loc = green.shape[1]
    freq_count = lax.axis_size("freq")
    freq_total = freq_loc * freq_count
    chains = chains_loc * freq_count
    forward_table = spectral_table(time_len, freq_total)
    inverse_table = forward_table.T
    green_re = green[0]
    green_im = green[1]
    upper_rows = jnp.concatenate([green_re, green_im], axis=2)
    lower_rows = jnp.concatenate([-green_im, green_re], axis=2)
    kernel = jnp.concatenate([upper_rows, lower_rows], axis=1)
    weights = jnp.concatenate([inv_noise, inv_noise], axis=1)
    temper_cols = temper[:, None, None]
    current = chain_state
    moment = second_moment
    for step_num in range(noise.shape[0]):
        low_state = current.astype(jnp.bfloat16)
        local_spec = jnp.dot(
            low_state.reshape(chains_loc * slab_rows, time_len),
            forward_table,
            preferred_element_type=jnp.float32,
        )
        local_spec = local_spec.astype(jnp.bfloat16).reshape(chains_loc, slab_rows, 2 * freq_total)
        spectrum = lax.all_to_all(local_spec, "freq", split_axis=2, concat_axis=0, tiled=True)
        mixed_spec = (
            spectrum.reshape(chains, slab_rows, freq_loc, 2)
            .transpose(2, 0, 3, 1)
            .reshape(freq_loc, chains, 2 * slab_rows)
        )
        partial_data = jnp.einsum(
            "fcq,fqs->fcs", mixed_spec, kernel, preferred_element_type=jnp.float32
        )
        predicted = lax.psum(partial_data.astype(jnp.bfloat16), "param").astype(jnp.float32)
        weighted = (weights[:, None, :] * (predicted - observed[:, None, :])).astype(jnp.bfloat16)
        adjoint = jnp.einsum(
            "fcs,fqs->fcq", weighted, kernel, preferred_element_type=jnp.float32
        ).astype(jnp.bfloat16)
        adjoint = (
            adjoint.reshape(freq_loc, chains, 2, slab_rows)
            .transpose(1, 3, 0, 2)
            .reshape(chains, slab_rows, 2 * freq_loc)
        )
        own_adjoint = lax.all_to_all(adjoint, "freq", split_axis=0, concat_axis=2, tiled=True)
        gradient = jnp.dot(
            own_adjoint.reshape(chains_loc * slab_rows, 2 * freq_total),
            inverse_table,
            preferred_element_type=jnp.float32,
        )
        gradient = gradient.reshape(chains_loc, slab_rows, time_len)
        drift_term = temper_cols * gradient + current
        moment = decay_rate * moment + (1.0 - decay_rate) * drift_term * drift_term
        precondition = lax.rsqrt(moment)
        current = (
            current
            - step_length * precondition * drift_term
            + math.sqrt(2.0 * step_length) * jnp.sqrt(precondition) * noise[step_num]
        )
    return (current, moment)


def solution(mesh):
    return jax.shard_map(
        on_device,
        mesh=mesh,
        in_specs=(
            P("freq", "param", None),
            P("freq", "param", None),
            P(None, "freq", "param", None),
            P(None, "freq", "param", None),
            P("freq", None),
            P("freq", None),
            P("freq"),
        ),
        out_specs=(P("freq", "param", None), P("freq", "param", None)),
        check_vma=False,
    )
```

```python
import functools
import math

import jax
import jax.numpy as jnp
from jax import lax
from jax.experimental import pallas as pl
from jax.experimental.pallas import tpu as pltpu
from jax.sharding import PartitionSpec as P

decay_rate = 0.9
step_length = 0.5
MESH = pl.DeviceIdType.MESH
LANES = 128
GROUPS = 2
CHUNK_FREQS = 2
CORE_LAG = 2
HOP_LAG = 5
GATHER_LAG = 3
ADJ_LAG = 8
SPEC_LAG = 9
TABLE_ROWS = 16
UPDATE_CHAINS = 4
FINAL_CHAINS = 2


def spectral_table(time_len, freq_total):
    time_index = jnp.arange(time_len, dtype=jnp.int32)[:, None]
    wave_number = jnp.arange(freq_total, dtype=jnp.int32)[None, :] + 1
    phase_angle = (time_index * wave_number % time_len).astype(jnp.float32) * (
        2.0 * math.pi / time_len
    )
    columns_table = jnp.stack([jnp.cos(phase_angle), -jnp.sin(phase_angle)], axis=-1).reshape(
        time_len, 2 * freq_total
    )
    return (columns_table / math.sqrt(time_len)).astype(jnp.bfloat16)


def steps_kernel(
    freq_count, param_count, chunk_freqs,
    temper_hbm, obs_hbm, inv_hbm, state_hbm, moment_hbm, noise_hbm, green_hbm,
    adj_all, state, moment, push, table_ref,
    temper_ref, obs_all, inv_all, obs_rows, inv_rows, green, noise, rows32, spec, field, acc,
    core_out, core_in, up_out, up_in, down_out, down_in, wtd, adj,
    small_sem, state_sem, green_sem, moment_sem, noise_sem, push_sem, spec_send, spec_recv,
    line_send, line_recv, adj_send, adj_recv,
):
    freq_me = lax.axis_index("freq")
    param_me = lax.axis_index("param")
    steps = noise.shape[0]
    groups = acc.shape[0]
    freq_loc = field.shape[1]
    rows, slab = field.shape[3], field.shape[4]
    group_chains = rows // 2
    all_rows, half = acc.shape[2], acc.shape[3]
    sensors = 2 * half
    col_blocks = slab // LANES
    columns = table_ref.shape[0]
    chunks = freq_loc // chunk_freqs
    turns = group_chains // UPDATE_CHAINS
    line = param_count // 2
    core = lax.rem(param_me, 2)
    chip = param_me // 2
    core_peer = param_me + 1 - 2 * core
    above, below = param_me + 2, param_me - 2
    has_above, has_below = chip < line - 1, chip > 0
    peers = pl.ds(0, freq_count - 1)

    def freq_peer(d):
        return lax.rem(freq_me + d, freq_count)

    barrier = pltpu.get_barrier_semaphore()
    for d in range(1, freq_count):
        pl.semaphore_signal(barrier, inc=1, device_id={"freq": freq_peer(d)}, device_id_type=MESH)
    pl.semaphore_signal(barrier, inc=1, device_id={"param": core_peer}, device_id_type=MESH)

    @pl.when(has_above)
    def _():
        pl.semaphore_signal(barrier, inc=1, device_id={"param": above}, device_id_type=MESH)

    @pl.when(has_below)
    def _():
        pl.semaphore_signal(barrier, inc=1, device_id={"param": below}, device_id_type=MESH)

    def state_copy(c):
        return pltpu.make_async_copy(state_hbm.at[c], state.at[c], state_sem.at[c])

    def green_copy(f):
        return pltpu.make_async_copy(green_hbm.at[:, f], green.at[f], green_sem.at[f])

    def moment_copy(c):
        return pltpu.make_async_copy(moment_hbm.at[c], moment.at[c], moment_sem.at[0])

    def noise_copy(s, c):
        return pltpu.make_async_copy(noise_hbm.at[s, c], noise.at[s, c], noise_sem.at[s])

    def push_copy():
        left = pl.ds((groups - 1) * group_chains, group_chains)
        return pltpu.make_async_copy(noise_hbm.at[steps - 1, left], push, push_sem.at[0])

    def small_copy(k, src, dst):
        return pltpu.make_async_copy(src, dst, small_sem.at[k])

    def arrived(ref, sem):
        pltpu.make_async_copy(ref, ref, sem).wait()

    def freqs_of(i):
        return pl.ds(i * chunk_freqs, chunk_freqs)

    def spec_copy(q, g, i, d):
        return pltpu.make_async_remote_copy(
            src_ref=spec.at[q, freq_peer(d), freqs_of(i)],
            dst_ref=field.at[q, freqs_of(i), freq_me],
            send_sem=spec_send.at[0],
            recv_sem=spec_recv.at[g, i],
            device_id={"freq": freq_peer(d)},
            device_id_type=MESH,
        )

    def adj_copy(q, g, i, d):
        return pltpu.make_async_remote_copy(
            src_ref=adj.at[q, freqs_of(i), freq_peer(d)],
            dst_ref=adj_all.at[q, freq_me, freqs_of(i)],
            send_sem=adj_send.at[0],
            recv_sem=adj_recv.at[g],
            device_id={"freq": freq_peer(d)},
            device_id_type=MESH,
        )

    def param_copy(k, g, i, src, dst, peer):
        return pltpu.make_async_remote_copy(
            src_ref=src.at[freqs_of(i)],
            dst_ref=dst.at[freqs_of(i)],
            send_sem=line_send.at[k],
            recv_sem=line_recv.at[k, g, i],
            device_id={"param": peer},
            device_id_type=MESH,
        )

    def core_reduce(q, g, i):
        return param_copy(0, g, i, core_out.at[q], core_in.at[q], core_peer)

    def core_gather(q, g, i):
        return param_copy(1, g, i, wtd.at[q, core], wtd.at[q, core], core_peer)

    def up_copy(q, g, i):
        return param_copy(2, g, i, up_out.at[q], up_in.at[q], above)

    def down_copy(q, g, i):
        return param_copy(3, g, i, down_out.at[q], down_in.at[q], below)

    def transform(g, k, low):
        dims = (((1,), (1,)), ((), ()))
        result = lax.dot_general(table_ref[...], low, dims, preferred_element_type=jnp.float32)
        for b in range(col_blocks):
            block = result[:, b * LANES : (b + 1) * LANES]
            rows32[g, b, pl.ds(k, columns, stride=group_chains)] = block

    def send_spectrum(q, g):
        @pl.loop(0, chunks)
        def _(i):
            for d in range(freq_count):
                for e in range(chunk_freqs):
                    f = i * chunk_freqs + e
                    first = pl.multiple_of((freq_peer(d) * freq_loc + f) * rows, rows)
                    pieces = [rows32[g, b, pl.ds(first, rows)] for b in range(col_blocks)]
                    tile = jnp.concatenate(pieces, axis=1).astype(jnp.bfloat16)
                    if d == 0:
                        field[q, f, freq_me] = tile
                    else:
                        spec[q, freq_peer(d), f] = tile
            for d in range(1, freq_count):
                spec_copy(q, g, i, d).start()

    @pl.loop(0, group_chains)
    def _(c):
        state_copy(c).start()

    smalls = ((temper_hbm, temper_ref), (obs_hbm, obs_all), (inv_hbm, inv_all))
    for k, (src, dst) in enumerate(smalls):
        small_copy(k, src, dst).start()

    fill_table(table_ref)
    met = has_above.astype(jnp.int32) + has_below.astype(jnp.int32)
    for g in range(groups):
        @pl.loop(0, group_chains)
        def _(k):
            c = g * group_chains + k
            state_copy(c).wait()
            if g < groups - 1:
                state_copy(c + group_chains).start()
            transform(g, k, state[c].astype(jnp.bfloat16))

        if g == groups - 1:
            @pl.loop(0, freq_loc)
            def _(f):
                green_copy(f).start()

            @pl.loop(0, groups * group_chains)
            def _(c):
                moment_copy(c).start()
                for s in range(steps - 1):
                    noise_copy(s, c).start()

            @pl.loop(0, (groups - 1) * group_chains)
            def _(c):
                noise_copy(steps - 1, c).start()

            push_copy().start()

        if g == 0:
            pl.semaphore_wait(barrier, freq_count + met)
        send_spectrum(g, g)

    for k, (src, dst) in enumerate(smalls):
        small_copy(k, src, dst).wait()
    for f in range(freq_loc):
        first = pl.multiple_of(core * half, half)
        inv_rows[f] = inv_all[f : f + 1, pl.ds(first, half)]
        for ri in range(2):
            first = pl.multiple_of(ri * sensors + core * half, half)
            target = obs_all[f : f + 1, pl.ds(first, half)]
            obs_rows[f, ri * group_chains : (ri + 1) * group_chains] = jnp.broadcast_to(
                target, (group_chains, half)
            )

    def turned(x, sign):
        wide = x.astype(jnp.float32).reshape(freq_count, rows, x.shape[-1])
        row = lax.broadcasted_iota(jnp.int32, wide.shape, 1)
        back = pltpu.roll(wide, group_chains, 1)
        flip = row < group_chains if sign > 0 else row >= group_chains
        return jnp.where(flip, -back, back).reshape(all_rows, x.shape[-1]).astype(jnp.bfloat16)

    def forward(s, n):
        g, i = lax.div(n, chunks), lax.rem(n, chunks)
        q = s * groups + g

        @pl.when((s == 0) & (g == 0))
        def _():
            for e in range(chunk_freqs):
                green_copy(i * chunk_freqs + e).wait()

        arrived(field.at[q, freqs_of(i), peers], spec_recv.at[g, i])
        for e in range(chunk_freqs):
            f = i * chunk_freqs + e
            wide = field[q, f].astype(jnp.float32).reshape(all_rows, slab)
            both = jnp.concatenate([wide.astype(jnp.bfloat16), turned(wide, 1)], axis=1)
            weights = green[f].reshape(2 * slab, sensors)
            data = jnp.dot(both, weights, preferred_element_type=jnp.float32)
            low, high = data[:, :half], data[:, half:]
            acc[g, f] = jnp.where(core == 0, low, high)
            core_out[q, f] = jnp.where(core == 0, high, low).astype(jnp.bfloat16)
        core_reduce(q, g, i).start()

    def merge(s, n):
        g, i = lax.div(n, chunks), lax.rem(n, chunks)
        q = s * groups + g
        core_reduce(q, g, i).wait_recv()
        total = acc[g, freqs_of(i)] + core_in[q, freqs_of(i)].astype(jnp.float32)
        acc[g, freqs_of(i)] = total

        @pl.when(chip == 0)
        def _():
            up_out[q, freqs_of(i)] = total.astype(jnp.bfloat16)
            up_copy(q, g, i).start()

        @pl.when(chip == line - 1)
        def _():
            down_out[q, freqs_of(i)] = total.astype(jnp.bfloat16)
            down_copy(q, g, i).start()

    def pass_up(s, n):
        g, i = lax.div(n, chunks), lax.rem(n, chunks)
        q = s * groups + g
        up_copy(q, g, i).wait_recv()
        total = acc[g, freqs_of(i)] + up_in[q, freqs_of(i)].astype(jnp.float32)
        up_out[q, freqs_of(i)] = total.astype(jnp.bfloat16)
        up_copy(q, g, i).start()

    def pass_down(s, n):
        g, i = lax.div(n, chunks), lax.rem(n, chunks)
        q = s * groups + g
        down_copy(q, g, i).wait_recv()
        total = acc[g, freqs_of(i)] + down_in[q, freqs_of(i)].astype(jnp.float32)
        down_out[q, freqs_of(i)] = total.astype(jnp.bfloat16)
        down_copy(q, g, i).start()

    def weigh(s, n):
        g, i = lax.div(n, chunks), lax.rem(n, chunks)
        q = s * groups + g

        @pl.when(chip == line - 1)
        def _():
            up_copy(q, g, i).wait_recv()

        @pl.when(chip == 0)
        def _():
            down_copy(q, g, i).wait_recv()

        @pl.when(has_below)
        def _():
            acc[g, freqs_of(i)] += up_in[q, freqs_of(i)].astype(jnp.float32)

        @pl.when(has_above)
        def _():
            acc[g, freqs_of(i)] += down_in[q, freqs_of(i)].astype(jnp.float32)

        for e in range(chunk_freqs):
            f = i * chunk_freqs + e
            apart = acc[g, f].reshape(freq_count, rows, half) - obs_rows[f][None]
            scaled = inv_rows[f][None] * apart
            wtd[q, core, f] = scaled.reshape(all_rows, half).astype(jnp.bfloat16)
        core_gather(q, g, i).start()

    def backward(s, n):
        g, i = lax.div(n, chunks), lax.rem(n, chunks)
        q = s * groups + g
        core_gather(q, g, i).wait_recv()
        dims = (((1,), (1,)), ((), ()))
        for e in range(chunk_freqs):
            f = i * chunk_freqs + e
            w = jnp.concatenate([wtd[q, 0, f], wtd[q, 1, f]], axis=1)
            first = lax.dot_general(w, green[f, 0], dims, preferred_element_type=jnp.float32)
            second = lax.dot_general(
                turned(w, -1), green[f, 1], dims, preferred_element_type=jnp.float32
            )
            back = (first + second).reshape(freq_count, rows, slab)
            adj[q, f] = back.astype(jnp.bfloat16)
            adj_all[q, freq_me, f] = adj[q, f, freq_me]
        for d in range(1, freq_count):
            adj_copy(q, g, i, d).start()

    def update(s, n):
        g, k = lax.div(n, chunks), lax.rem(n, chunks)
        q = s * groups + g
        going_on = s < steps - 1

        @pl.when((k < turns) & (going_on | (g < groups - 1)))
        def _():
            @pl.when(k == 0)
            def _():
                arrived(adj_all.at[q, peers], adj_recv.at[g])
                widen(adj_all.at[q], rows32.at[g])

                @pl.when(g == 0)
                def _():
                    @pl.when(s == 0)
                    def _():
                        arrived(moment, moment_sem.at[0])

                    @pl.when(going_on)
                    def _():
                        arrived(noise.at[s], noise_sem.at[s])

                    @pl.when(s == steps - 1)
                    def _():
                        read = pl.ds(0, (groups - 1) * group_chains)
                        arrived(noise.at[s, read], noise_sem.at[s])

            lows = []
            for e in range(UPDATE_CHAINS):
                here = k * UPDATE_CHAINS + e
                low = advance(
                    here, g * group_chains + here, rows32.at[g], table_ref, temper_ref,
                    state, moment, noise.at[s], state, moment,
                )
                lows.append(low)

            @pl.when(going_on)
            def _():
                for e in range(UPDATE_CHAINS):
                    transform(g, k * UPDATE_CHAINS + e, lows[e])

            @pl.when(going_on & (k == turns - 1))
            def _():
                send_spectrum(q + groups, g)

    span = groups * chunks
    up_lag = CORE_LAG + HOP_LAG * chip
    down_lag = CORE_LAG + HOP_LAG * (line - 1 - chip)
    weigh_lag = jnp.maximum(up_lag, down_lag)
    back_lag = CORE_LAG + HOP_LAG * (line - 1) + GATHER_LAG
    update_lag = back_lag + chunks - 1 + ADJ_LAG
    period = max(update_lag + turns - 1 + SPEC_LAG, span)
    inside = has_above & has_below
    total_ticks = (steps - 1) * period + max(
        span + back_lag, update_lag + (groups - 2) * chunks + turns
    )

    @pl.loop(0, total_ticks)
    def _(tick):
        def stage(lag, work, allowed=None):
            since = jnp.maximum(tick - lag, 0)
            s = lax.div(since, period)
            n = since - s * period
            due = (tick >= lag) & (s < steps) & (n < span)

            @pl.when(due if allowed is None else due & allowed)
            def _():
                work(s, n)

        stage(0, forward)
        stage(weigh_lag + GATHER_LAG, backward)
        stage(CORE_LAG, merge)
        stage(up_lag, pass_up, inside)
        stage(down_lag, pass_down, inside)
        stage(weigh_lag, weigh)
        stage(update_lag, update)

    last = steps * groups - 1
    push_copy().wait()
    arrived(adj_all.at[last, peers], adj_recv.at[groups - 1])
    arrived(spec.at[:, peers], spec_send.at[0])
    arrived(adj.at[:, :, peers], adj_send.at[0])
    for k in range(2):
        arrived(core_out, line_send.at[k])

    @pl.when(has_above)
    def _():
        arrived(core_out, line_send.at[2])

    @pl.when(has_below)
    def _():
        arrived(core_out, line_send.at[3])


def fill_table(table_ref):
    columns, time_len = table_ref.shape

    @pl.loop(0, columns // TABLE_ROWS)
    def _(i):
        first = pl.multiple_of(i * TABLE_ROWS, TABLE_ROWS)
        column = lax.broadcasted_iota(jnp.int32, (TABLE_ROWS, time_len), 0) + first
        time_index = lax.broadcasted_iota(jnp.int32, (TABLE_ROWS, time_len), 1)
        turn = time_index * ((column >> 1) + 1) + (column & 1) * (time_len // 4)
        phase_angle = (turn & (time_len - 1)).astype(jnp.float32) * (2.0 * math.pi / time_len)
        rows = jnp.cos(phase_angle) / math.sqrt(time_len)
        table_ref[pl.ds(first, TABLE_ROWS)] = rows.astype(jnp.bfloat16)


def widen(adj, rows32):
    freq_count, freq_loc, rows, slab = adj.shape

    @pl.loop(0, freq_count)
    def _(j):
        for f in range(freq_loc):
            first = pl.multiple_of((j * freq_loc + f) * rows, rows)
            tile = adj[j, f].astype(jnp.float32)
            for b in range(slab // LANES):
                rows32[b, pl.ds(first, rows)] = tile[:, b * LANES : (b + 1) * LANES]


def advance(k, c, rows32, table_ref, temper_ref, state, moment, push, new_state, new_moment):
    columns, group_chains = table_ref.shape[0], rows32.shape[1] // table_ref.shape[0]
    pieces = [
        rows32[b, pl.ds(k, columns, stride=group_chains)] for b in range(rows32.shape[0])
    ]
    mine = jnp.concatenate(pieces, axis=1).T.astype(jnp.bfloat16)
    gradient = jnp.dot(mine, table_ref[...], preferred_element_type=jnp.float32)
    current = state[c]
    drift_term = temper_ref[c] * gradient + current
    spread = moment[c]
    spread = decay_rate * spread + (1.0 - decay_rate) * drift_term * drift_term
    precondition = lax.rsqrt(spread)
    kick = math.sqrt(2.0 * step_length) * lax.rsqrt(precondition) * push[c]
    current = current - precondition * (step_length * drift_term - kick)
    new_state[c] = current
    new_moment[c] = spread
    return current.astype(jnp.bfloat16)


def final_kernel(
    table_ref, temper_ref, adj_all, state, moment, push, state_hbm, moment_hbm,
    rows32, new_state, new_moment, state_sem, moment_sem,
):
    last = adj_all.shape[0] - 1
    left = new_state.shape[0]
    done = state.shape[0] - left

    def state_copy(k):
        c = done + k
        return pltpu.make_async_copy(new_state.at[k], state_hbm.at[c], state_sem.at[c])

    def moment_copy(k):
        c = done + k
        return pltpu.make_async_copy(new_moment.at[k], moment_hbm.at[c], moment_sem.at[c])

    def done_state_copy(c):
        return pltpu.make_async_copy(state.at[c], state_hbm.at[c], state_sem.at[c])

    def done_moment_copy(c):
        return pltpu.make_async_copy(moment.at[c], moment_hbm.at[c], moment_sem.at[c])

    @pl.loop(0, done)
    def _(c):
        done_state_copy(c).start()
        done_moment_copy(c).start()

    widen(adj_all.at[last], rows32)

    @pl.loop(0, left // FINAL_CHAINS)
    def _(i):
        here = pl.ds(done, left)
        for e in range(FINAL_CHAINS):
            k = i * FINAL_CHAINS + e
            advance(
                k, k, rows32, table_ref, temper_ref.at[here], state.at[here], moment.at[here],
                push, new_state, new_moment,
            )
            state_copy(k).start()
            moment_copy(k).start()

    @pl.loop(0, done)
    def _(c):
        done_state_copy(c).wait()
        done_moment_copy(c).wait()

    @pl.loop(0, left)
    def _(k):
        state_copy(k).wait()
        moment_copy(k).wait()


def fits_kernel(chain_shape, green_shape):
    chains_loc, slab = chain_shape[0], chain_shape[1]
    param_count = lax.axis_size("param")
    return (
        chains_loc % GROUPS == 0
        and 2 * (chains_loc // GROUPS) % 8 == 0
        and slab % LANES == 0
        and chain_shape[2] % LANES == 0
        and chain_shape[2] & (chain_shape[2] - 1) == 0
        and 2 * green_shape[1] * lax.axis_size("freq") % TABLE_ROWS == 0
        and green_shape[3] % (2 * LANES) == 0
        and green_shape[1] % CHUNK_FREQS == 0
        and green_shape[1] // CHUNK_FREQS >= chains_loc // GROUPS
        and chains_loc // GROUPS % UPDATE_CHAINS == 0
        and chains_loc // GROUPS % FINAL_CHAINS == 0
        and param_count == 8
        and lax.axis_size("freq") > 1
    )


def kernel_steps(chain_state, second_moment, noise, green, observed, inv_noise, temper):
    chains_loc, slab, time_len = chain_state.shape
    freq_loc, sensors = green.shape[1], green.shape[3]
    steps = noise.shape[0]
    freq_count, param_count = lax.axis_size("freq"), lax.axis_size("param")
    columns = 2 * freq_loc * freq_count
    chunks = freq_loc // CHUNK_FREQS
    group_chains = chains_loc // GROUPS
    rows, half = 2 * group_chains, sensors // 2
    all_rows = freq_count * rows
    items = steps * GROUPS
    bf16, f32 = jnp.bfloat16, jnp.float32
    dma = pltpu.SemaphoreType.DMA
    vmem = pl.BlockSpec(memory_space=pltpu.VMEM)
    smem = pl.BlockSpec(memory_space=pltpu.SMEM)
    hbm = pl.BlockSpec(memory_space=pltpu.HBM)
    line_buf = pltpu.VMEM((items, freq_loc, all_rows, half), bf16)
    rows32 = (slab // LANES, columns * group_chains, LANES)
    part = (group_chains, slab, time_len)
    operands = [
        pltpu.with_memory_space_constraint(x, pltpu.HBM)
        for x in (temper, observed, inv_noise, chain_state, second_moment, noise, green)
    ]
    adj_all, state, moment, push, table = pl.pallas_call(
        functools.partial(steps_kernel, freq_count, param_count, CHUNK_FREQS),
        out_shape=[
            jax.ShapeDtypeStruct((items, freq_count, freq_loc, rows, slab), bf16),
            jax.ShapeDtypeStruct(chain_state.shape, f32),
            jax.ShapeDtypeStruct(chain_state.shape, f32),
            jax.ShapeDtypeStruct(part, f32),
            jax.ShapeDtypeStruct((columns, time_len), bf16),
        ],
        in_specs=[hbm, hbm, hbm, hbm, hbm, hbm, hbm],
        out_specs=[vmem, vmem, vmem, vmem, vmem],
        scratch_shapes=[
            pltpu.SMEM(temper.shape, f32),
            pltpu.VMEM(observed.shape, f32),
            pltpu.VMEM(inv_noise.shape, f32),
            pltpu.VMEM((freq_loc, rows, half), f32),
            pltpu.VMEM((freq_loc, 1, half), f32),
            pltpu.VMEM((freq_loc, 2, slab, sensors), bf16),
            pltpu.VMEM((steps,) + chain_state.shape, f32),
            pltpu.VMEM((GROUPS,) + rows32, f32),
            pltpu.VMEM((items, freq_count, freq_loc, rows, slab), bf16),
            pltpu.VMEM((items, freq_loc, freq_count, rows, slab), bf16),
            pltpu.VMEM((GROUPS, freq_loc, all_rows, half), f32),
            line_buf, line_buf, line_buf, line_buf, line_buf, line_buf,
            pltpu.VMEM((items, 2, freq_loc, all_rows, half), bf16),
            pltpu.VMEM((items, freq_loc, freq_count, rows, slab), bf16),
            dma((3,)),
            dma((chains_loc,)),
            dma((freq_loc,)),
            dma((1,)),
            dma((steps,)),
            dma((1,)),
            dma((1,)),
            dma((GROUPS, chunks)),
            dma((4,)),
            dma((4, GROUPS, chunks)),
            dma((1,)),
            dma((GROUPS,)),
        ],
        compiler_params=pltpu.CompilerParams(
            collective_id=0, has_side_effects=True, vmem_limit_bytes=36 * 2**20
        ),
    )(*operands)
    return pl.pallas_call(
        final_kernel,
        out_shape=[
            jax.ShapeDtypeStruct(chain_state.shape, f32),
            jax.ShapeDtypeStruct(chain_state.shape, f32),
        ],
        in_specs=[vmem, smem, vmem, vmem, vmem, vmem],
        out_specs=[hbm, hbm],
        scratch_shapes=[
            pltpu.VMEM(rows32, f32),
            pltpu.VMEM(part, f32),
            pltpu.VMEM(part, f32),
            dma((chains_loc,)),
            dma((chains_loc,)),
        ],
        compiler_params=pltpu.CompilerParams(vmem_limit_bytes=8 * 2**20),
    )(table, temper, adj_all, state, moment, push)


def on_device(chain_state, second_moment, noise, green, observed, inv_noise, temper):
    if fits_kernel(chain_state.shape, green.shape):
        return kernel_steps(
            chain_state, second_moment, noise, green, observed, inv_noise, temper
        )
    chains_loc, slab_rows, time_len = chain_state.shape
    freq_loc = green.shape[1]
    freq_count = lax.axis_size("freq")
    freq_total = freq_loc * freq_count
    chains = chains_loc * freq_count
    forward_table = spectral_table(time_len, freq_total)
    inverse_table = forward_table.T
    green_re = green[0]
    green_im = green[1]
    upper_rows = jnp.concatenate([green_re, green_im], axis=2)
    lower_rows = jnp.concatenate([-green_im, green_re], axis=2)
    kernel = jnp.concatenate([upper_rows, lower_rows], axis=1)
    weights = jnp.concatenate([inv_noise, inv_noise], axis=1)
    temper_cols = temper[:, None, None]
    current = chain_state
    moment = second_moment
    for step_num in range(noise.shape[0]):
        low_state = current.astype(jnp.bfloat16)
        local_spec = jnp.dot(
            low_state.reshape(chains_loc * slab_rows, time_len),
            forward_table,
            preferred_element_type=jnp.float32,
        )
        local_spec = local_spec.astype(jnp.bfloat16).reshape(chains_loc, slab_rows, 2 * freq_total)
        spectrum = lax.all_to_all(local_spec, "freq", split_axis=2, concat_axis=0, tiled=True)
        mixed_spec = (
            spectrum.reshape(chains, slab_rows, freq_loc, 2)
            .transpose(2, 0, 3, 1)
            .reshape(freq_loc, chains, 2 * slab_rows)
        )
        partial_data = jnp.einsum(
            "fcq,fqs->fcs", mixed_spec, kernel, preferred_element_type=jnp.float32
        )
        predicted = lax.psum(partial_data.astype(jnp.bfloat16), "param").astype(jnp.float32)
        weighted = (weights[:, None, :] * (predicted - observed[:, None, :])).astype(jnp.bfloat16)
        adjoint = jnp.einsum(
            "fcs,fqs->fcq", weighted, kernel, preferred_element_type=jnp.float32
        ).astype(jnp.bfloat16)
        adjoint = (
            adjoint.reshape(freq_loc, chains, 2, slab_rows)
            .transpose(1, 3, 0, 2)
            .reshape(chains, slab_rows, 2 * freq_loc)
        )
        own_adjoint = lax.all_to_all(adjoint, "freq", split_axis=0, concat_axis=2, tiled=True)
        gradient = jnp.dot(
            own_adjoint.reshape(chains_loc * slab_rows, 2 * freq_total),
            inverse_table,
            preferred_element_type=jnp.float32,
        )
        gradient = gradient.reshape(chains_loc, slab_rows, time_len)
        drift_term = temper_cols * gradient + current
        moment = decay_rate * moment + (1.0 - decay_rate) * drift_term * drift_term
        precondition = lax.rsqrt(moment)
        current = (
            current
            - step_length * precondition * drift_term
            + math.sqrt(2.0 * step_length) * jnp.sqrt(precondition) * noise[step_num]
        )
    return (current, moment)


def solution(mesh):
    return jax.shard_map(
        on_device,
        mesh=mesh,
        in_specs=(
            P("freq", "param", None),
            P("freq", "param", None),
            P(None, "freq", "param", None),
            P(None, "freq", "param", None),
            P("freq", None),
            P("freq", None),
            P("freq"),
        ),
        out_specs=(P("freq", "param", None), P("freq", "param", None)),
        check_vma=False,
    )
```
